256 devices in a mesh: feat: 128 (over y, x, z), samp: 2 (over core).
Axes of the slice: x: 4, y: 4, z: 8, core: 2. Of those that a mesh axis runs over, the one named last changes fastest.
Arguments:
- spectra: bfloat16 [131072, 512], P('feat', 'samp'), may hold values from -6 to 6
- pair_blocks: int32 [4096, 2], P('feat'), may hold values from -1 to 511, as said below
- windows: int32 [512, 2], replicated, may hold values from 0 to 20918, as said below
Outputs:
- corr: float32 [4096, 256, 256], P(('feat', 'samp'))
- profiles: bfloat16 [131072, 512], P('feat', 'samp')
The draws below stay inside these ranges and needn't reach their ends.
Inputs may be any that keep to these rules, and one draw needn't show every extreme that they name: `pair_blocks`: slots lie in groups of 8; slot s of the device at index d along feat is in group g = s // 8. A live entry (i, j) has block i among the 4 blocks of device d and block j among those of device d + g, with i <= j in group 0; no pair appears twice; unused slots hold -1 in both columns. At most 8 slots of a group are live, and some group has all 8 live. `windows`: column 0 is a block's first retention index and column 1 its last, which is at least 20 larger.
All inputs are finite; a program needn't handle non-finite values.
Results may differ from the reference program's by a relative error of at most 0.0075.
Values may be sent and summed in bfloat16 or wider, within the bound.
A program may use at most 64 MiB of HBM per device.

```python
import jax
import jax.numpy as jnp
import numpy as np
from jax import lax

BS = 256
BLK_DEV = 4
CAP = 8
REACH = 3
SLOTS = 32
SAMPLES = 512
NBLK = 512
FEATS = 131072
NPAIR = 4096


def draw_pair_blocks(key, part):
    nfeat = NBLK // BLK_DEV
    upper = [(a, b) for a in range(BLK_DEV) for b in range(BLK_DEV) if a <= b]
    every = [(a, b) for a in range(BLK_DEV) for b in range(BLK_DEV)]
    upper_a = jnp.array(np.array([p[0] for p in upper], dtype=np.int32))
    upper_b = jnp.array(np.array([p[1] for p in upper], dtype=np.int32))
    every_a = jnp.array(np.array([p[0] for p in every], dtype=np.int32))
    every_b = jnp.array(np.array([p[1] for p in every], dtype=np.int32))
    count_upper = len(upper)
    count_every = len(every)

    def one_group(index):
        device = index // (REACH + 1)
        group = index % (REACH + 1)
        local = jax.random.fold_in(key, index)
        order_upper = jax.random.permutation(jax.random.fold_in(local, 1), count_upper)[:CAP]
        order_every = jax.random.permutation(jax.random.fold_in(local, 2), count_every)[:CAP]
        first_local = jnp.where(group == 0, upper_a[order_upper], every_a[order_every])
        second_local = jnp.where(group == 0, upper_b[order_upper], every_b[order_every])
        livecount = jax.random.randint(jax.random.fold_in(local, 3), (), 2, CAP + 1)
        livecount = jnp.where((device == 0) & (group == 1), CAP, livecount)
        livecount = jnp.where(device + group >= nfeat, 0, livecount)
        alive = jnp.arange(CAP) < livecount
        first = jnp.where(alive, device * BLK_DEV + first_local, -1)
        second = jnp.where(alive, (device + group) * BLK_DEV + second_local, -1)
        return jnp.stack([first, second], axis=1)
    table = jax.vmap(one_group)(jnp.arange(nfeat * (REACH + 1)))
    return table.reshape(nfeat * (REACH + 1) * CAP, 2).astype(jnp.int32)


def draw_windows(key, part):
    blocks = jnp.arange(NBLK, dtype=jnp.int32)
    start = 40 * blocks + jax.random.randint(jax.random.fold_in(key, 11), (NBLK,), 0, 40)
    extent = jax.random.randint(jax.random.fold_in(key, 12), (NBLK,), 20, 400)
    return jnp.stack([start, start + extent], axis=1).astype(jnp.int32)


def levels(key, dims, shards, smallest, top_value):
    gain, own = 1.0, jax.random.fold_in(key, 6)
    for position, blocks in shards:
        draws = jnp.exp(jax.random.uniform(jax.random.fold_in(own, position), (blocks,), jnp.float32, smallest / len(shards), top_value / len(shards)))
        gain = gain * jnp.repeat(draws, dims[position] // blocks).reshape([-1 if axis == position else 1 for axis in range(len(dims))])
    return gain


def gaussian(stream_key, shape, deviation, most, pieces=(), kind=jnp.bfloat16):
    values = deviation * jax.random.normal(stream_key, shape, jnp.float32)
    if pieces:
        values = values * levels(stream_key, shape, pieces, -0.22, 0.18)
    return jnp.clip(values, -most, most).astype(kind)


def setup_inputs(seed: int = 0) -> dict:
    keys = jax.random.split(jax.random.key(seed), 4)
    spectra = gaussian(keys[0], (FEATS, SAMPLES), 1.0, 6.0, ((0, 128), (1, 2)))
    pair_blocks = draw_pair_blocks(jax.random.fold_in(keys[3], 71), 0)
    windows = draw_windows(jax.random.fold_in(keys[3], 71), 0)
    return {"spectra": spectra, "pair_blocks": pair_blocks, "windows": windows}


def reference(spectra, pair_blocks, windows):
    values = spectra.astype(jnp.float32)
    mean = lax.optimization_barrier(jnp.sum(values, axis=1)) / SAMPLES
    var = lax.optimization_barrier(jnp.sum(values * values, axis=1)) / SAMPLES - mean * mean
    inv = lax.rsqrt(var + 1e-05)
    z = ((values - mean[:, None]) * inv[:, None]).astype(jnp.bfloat16)
    zb = z.reshape(NBLK, BS, SAMPLES)
    first = pair_blocks[:, 0]
    second = pair_blocks[:, 1]
    live = first >= 0
    ia = jnp.maximum(first, 0)
    ja = jnp.maximum(second, 0)
    lo_i = windows[ia, 0]
    hi_i = windows[ia, 1]
    lo_j = windows[ja, 0]
    hi_j = windows[ja, 1]
    intersection = jnp.maximum(jnp.minimum(hi_i, hi_j) - jnp.maximum(lo_i, lo_j), 0)
    weight = (intersection + 16).astype(jnp.float32) / (hi_i - lo_i + hi_j - lo_j + 16).astype(jnp.float32)
    weight = jnp.where(live, weight, jnp.float32(0.0))

    def tile_of(args):
        ci, cj, cw = args
        gram = jnp.einsum('pfs,pgs->pfg', zb[ci].astype(jnp.float32), zb[cj].astype(jnp.float32))
        return gram * (cw / SAMPLES)[:, None, None]
    corr = lax.map(tile_of, (ia.reshape(-1, SLOTS), ja.reshape(-1, SLOTS), weight.reshape(-1, SLOTS)))
    tiles = corr.astype(jnp.bfloat16)
    corr = corr.reshape(NPAIR, BS, BS)

    def accumulate(acc, args):
        ci, cj, ct = args
        ct32 = ct.astype(jnp.float32)
        ahead = jnp.einsum('pfg,pgs->pfs', ct32, zb[cj].astype(jnp.float32))
        acc = acc.at[ci].add(ahead)
        differ = (ci != cj).astype(jnp.float32)
        behind = jnp.einsum('pfg,pfs->pgs', ct32, zb[ci].astype(jnp.float32)) * differ[:, None, None]
        acc = acc.at[cj].add(behind)
        return (acc, None)
    acc, _ = lax.scan(accumulate, zb.astype(jnp.float32), (ia.reshape(-1, SLOTS), ja.reshape(-1, SLOTS), tiles))
    profiles = acc.astype(jnp.bfloat16).reshape(FEATS, SAMPLES)
    return (corr, profiles)
```

```python
import functools

import jax
import jax.numpy as jnp
from jax import lax
from jax.experimental import pallas as pl
from jax.experimental.pallas import tpu as pltpu
from jax.sharding import PartitionSpec as P

BS = 256
BLK_DEV = 4
CAP = 8
REACH = 3
SLOTS = 32
HOPS = REACH * BLK_DEV
SAMPLES = 512
MESH = pl.DeviceIdType.MESH
NT = (((1,), (1,)), ((), ()))


def pair_weights(pairs, windows, base, own_w, slot_w):
    lane = lax.broadcasted_iota(jnp.int32, (1, 128), 1)
    code = jnp.full((1, 128), -1, jnp.int32)
    numer = jnp.zeros((1, 128), jnp.int32)
    denom = jnp.ones((1, 128), jnp.int32)
    for p in range(SLOTS):
        i, j = pairs[0, p], pairs[1, p]
        live = i >= 0
        ia, ja = jnp.maximum(i, 0), jnp.maximum(j, 0)
        lo_i, hi_i = windows[0, ia], windows[1, ia]
        lo_j, hi_j = windows[0, ja], windows[1, ja]
        inter = jnp.maximum(jnp.minimum(hi_i, hi_j) - jnp.maximum(lo_i, lo_j), 0)
        near = i - base
        far = j - base - (p // CAP) * BLK_DEV
        here = lane == p
        code = jnp.where(here, jnp.where(live, near * BLK_DEV + far, -1), code)
        numer = jnp.where(here, jnp.where(live, inter + 16, 0), numer)
        denom = jnp.where(here, jnp.where(live, hi_i - lo_i + hi_j - lo_j + 16, 1), denom)
    weight = numer.astype(jnp.float32) / denom.astype(jnp.float32)
    row = lax.broadcasted_iota(jnp.int32, (16, 128), 0)
    wide = lax.broadcasted_iota(jnp.int32, (16, 128), 1)
    packed = jnp.zeros((16, 128), jnp.float32)
    for g in range(REACH + 1):
        hit = (row == code) & (wide // CAP == g)
        column = jnp.sum(jnp.where(hit, weight, 0.0), axis=1, keepdims=True)
        packed = jnp.where(wide // 32 == g, column, packed)
    own_w[...] = packed * (1.0 / SAMPLES)
    srow = lax.broadcasted_iota(jnp.int32, (SLOTS, 128), 0)
    swide = lax.broadcasted_iota(jnp.int32, (SLOTS, 128), 1)
    per_slot = jnp.sum(jnp.where(srow == swide, weight, 0.0), axis=1, keepdims=True)
    slot_w[...] = jnp.broadcast_to(per_slot, (SLOTS, 128))


def kernel(
    length,
    spectra, pairs, windows,
    corr, acc,
    z, ahead, behind, sib_ahead, sib_behind, sib_own, own_w, slot_w, far_w,
    send_a, recv_a, send_b, recv_b,
    send_sa, recv_sa, send_sb, recv_sb, send_so, recv_so, send_w, recv_w,
):
    me = lax.axis_index("feat")
    core = lax.axis_index("samp")
    right, left = lax.rem(me + 1, length), lax.rem(me + length - 1, length)
    to_left, to_right, to_sib = (left, core), (right, core), (me, 1 - core)

    barrier = pltpu.get_barrier_semaphore()
    for target in (to_left, to_right, to_sib):
        pl.semaphore_signal(barrier, inc=1, device_id=target, device_id_type=MESH)
    pair_weights(pairs, windows, me * BLK_DEV, own_w, slot_w)
    pl.semaphore_wait(barrier, 3)

    def remote(src, dst, send, recv, target):
        return pltpu.make_async_remote_copy(
            src_ref=src, dst_ref=dst, send_sem=send, recv_sem=recv,
            device_id=target, device_id_type=MESH,
        )

    def own_chunk(b):
        return spectra.at[pl.ds(b * BS, BS), :]

    def w_copy(h):
        source = own_w if h == 0 else far_w.at[h - 1]
        return remote(source, far_w.at[h], send_w.at[h], recv_w.at[h], to_right)

    def ahead_copy(m, source):
        return remote(source, ahead.at[m], send_a.at[m], recv_a.at[m], to_left)

    def behind_copy(m, source):
        return remote(source, behind.at[m], send_b.at[m], recv_b.at[m], to_right)

    def sib_ahead_copy(m):
        return remote(ahead.at[m], sib_ahead.at[m], send_sa.at[m], recv_sa.at[m], to_sib)

    def sib_behind_copy(m):
        return remote(behind.at[m], sib_behind.at[m], send_sb.at[m], recv_sb.at[m], to_sib)

    def sib_own_copy(b):
        return remote(own_chunk(b), sib_own.at[b], send_so.at[b], recv_so.at[b], to_sib)

    w_copy(0).start()
    for b in range(BLK_DEV):
        sib_own_copy(b).start()
        ahead_copy(b, own_chunk(b)).start()
        behind_copy(b, own_chunk(b)).start()

    def standardize(mine, other):
        x1, x2 = mine.astype(jnp.float32), other.astype(jnp.float32)
        total = jnp.sum(x1 + x2, axis=1, keepdims=True)
        squares = jnp.sum(x1 * x1 + x2 * x2, axis=1, keepdims=True)
        mean = total / SAMPLES
        var = squares / SAMPLES - mean * mean
        inv = lax.rsqrt(var + 1e-05)
        z1, z2 = (x1 - mean) * inv, (x2 - mean) * inv
        return jnp.concatenate([z1.astype(jnp.bfloat16), z2.astype(jnp.bfloat16)], axis=1)

    def gram(za, zc):
        return lax.dot_general(za, zc, NT, preferred_element_type=jnp.float32)

    def own_block(b, _):
        sib_own_copy(b).wait_recv()
        rows = pl.ds(pl.multiple_of(b * BS, BS), BS)
        zb = standardize(spectra[rows, :], sib_own[b])
        z[b] = zb
        acc[rows, :] = zb[:, :BS].astype(jnp.float32)
        return 0

    lax.fori_loop(0, BLK_DEV, own_block, 0)

    for a in range(BLK_DEV):
        tiles = []
        for c in range(BLK_DEV):
            r = min(a, c) * BLK_DEV + max(a, c)
            tiles.append((gram(z[a], z[c]) * own_w[r : r + 1, 0:1]).astype(jnp.bfloat16))
        halves = jnp.concatenate([z[c, :, :BS] for c in range(BLK_DEV)], axis=0)
        acc[a * BS : (a + 1) * BS, :] += jnp.dot(
            jnp.concatenate(tiles, axis=1), halves, preferred_element_type=jnp.float32
        )

    def slots_of_group(g, first_out):
        def one(q, _):
            p = g * CAP + q
            near = jnp.clip(pairs[0, p] - me * BLK_DEV, 0, BLK_DEV - 1)
            far = jnp.clip(pairs[1, p] - (me + g) * BLK_DEV, 0, BLK_DEV - 1)
            corr[first_out + q] = gram(z[near], z[g * BLK_DEV + far]) * slot_w[pl.ds(p, 1), 0:1]
            return 0

        lax.fori_loop(0, CAP, one, 0)

    @pl.when(core == 0)
    def _():
        slots_of_group(0, 0)

    def step(k, _):
        @pl.when(k < HOPS)
        def _():
            ahead_copy(k, ahead.at[k]).wait_recv()
            behind_copy(k, behind.at[k]).wait_recv()

            @pl.when(k < HOPS - BLK_DEV)
            def _():
                ahead_copy(k + BLK_DEV, ahead.at[k]).start()
                behind_copy(k + BLK_DEV, behind.at[k]).start()

            sib_ahead_copy(k).start()
            sib_behind_copy(k).start()
            for h in range(REACH):
                @pl.when(k == h * BLK_DEV)
                def _():
                    w_copy(h).wait_recv()
                    if h < REACH - 1:
                        w_copy(h + 1).start()

        @pl.when(k > 0)
        def _():
            m = k - 1
            g = m // BLK_DEV + 1
            c = m % BLK_DEV
            sib_ahead_copy(m).wait_recv()
            sib_behind_copy(m).wait_recv()
            za = standardize(ahead[m], sib_ahead[m])
            zb = standardize(behind[m], sib_behind[m])
            z[BLK_DEV + m] = za
            halves = jnp.concatenate([za[:, :BS], zb[:, :BS]], axis=0)
            picked = lax.broadcasted_iota(jnp.int32, (1, 128), 1) // 32 == g
            for a in range(BLK_DEV):
                wa = jnp.where(picked, own_w[pl.ds(a * BLK_DEV + c, 1), :], 0.0)
                wb = jnp.where(picked, far_w[g - 1, pl.ds(c * BLK_DEV + a, 1), :], 0.0)
                wa = jnp.max(wa, axis=1, keepdims=True)
                wb = jnp.max(wb, axis=1, keepdims=True)
                ta = (gram(z[a], za) * wa).astype(jnp.bfloat16)
                tb = (gram(z[a], zb) * wb).astype(jnp.bfloat16)
                acc[a * BS : (a + 1) * BS, :] += jnp.dot(
                    jnp.concatenate([ta, tb], axis=1), halves, preferred_element_type=jnp.float32
                )

            @pl.when((c == BLK_DEV - 1) & (core == g // 2))
            def _():
                slots_of_group(g, (g % 2) * CAP)

        return 0

    lax.fori_loop(0, HOPS + 1, step, 0)

    for h in range(REACH):
        w_copy(h).wait_send()

    def drain(m, _):
        ahead_copy(m, ahead.at[m]).wait_send()
        behind_copy(m, behind.at[m]).wait_send()
        sib_ahead_copy(m).wait_send()
        sib_behind_copy(m).wait_send()
        return 0

    lax.fori_loop(0, HOPS, drain, 0)
    for b in range(BLK_DEV):
        sib_own_copy(b).wait_send()


def body(spectra, pair_blocks, windows):
    length = lax.axis_size("feat")
    rows, width = spectra.shape
    vmem, smem = pl.BlockSpec(memory_space=pltpu.VMEM), pl.BlockSpec(memory_space=pltpu.SMEM)
    chunks = pltpu.VMEM((HOPS, BS, BS), jnp.bfloat16)
    many = pltpu.SemaphoreType.DMA((HOPS,))
    few = pltpu.SemaphoreType.DMA((BLK_DEV,))
    corr, acc = pl.pallas_call(
        functools.partial(kernel, length),
        out_shape=(
            jax.ShapeDtypeStruct((SLOTS // 2, BS, BS), jnp.float32),
            jax.ShapeDtypeStruct((rows, width), jnp.float32),
        ),
        in_specs=[vmem, smem, smem],
        out_specs=(vmem, vmem),
        scratch_shapes=[
            pltpu.VMEM((BLK_DEV + HOPS, BS, 2 * BS), jnp.bfloat16),
            chunks, chunks, chunks, chunks,
            pltpu.VMEM((BLK_DEV, BS, BS), jnp.bfloat16),
            pltpu.VMEM((16, 128), jnp.float32),
            pltpu.VMEM((SLOTS, 128), jnp.float32),
            pltpu.VMEM((REACH, 16, 128), jnp.float32),
            many, many, many, many,
            many, many, many, many,
            few, few,
            pltpu.SemaphoreType.DMA((REACH,)), pltpu.SemaphoreType.DMA((REACH,)),
        ],
        compiler_params=pltpu.CompilerParams(
            collective_id=0, has_side_effects=True, vmem_limit_bytes=40 << 20
        ),
    )(spectra, pair_blocks.T, windows.T)
    return corr * (1.0 / SAMPLES), acc.astype(jnp.bfloat16)


def solution(mesh):
    placed = (P("feat", "samp"), P("feat", None), P())
    return jax.shard_map(
        body,
        mesh=mesh,
        in_specs=placed,
        out_specs=(P(("feat", "samp"), None, None), P("feat", "samp")),
        check_vma=False,
    )
```

```python
import functools

import jax
import jax.numpy as jnp
from jax import lax
from jax.experimental import pallas as pl
from jax.experimental.pallas import tpu as pltpu
from jax.sharding import PartitionSpec as P

BS = 256
BLK_DEV = 4
CAP = 8
REACH = 3
SLOTS = 32
HOPS = REACH * BLK_DEV
LAST = HOPS - 1
HALF = BS // 2
COLUMN = 8
SAMPLES = 512
MESH = pl.DeviceIdType.MESH
NT = (((1,), (1,)), ((), ()))


def pair_weights(pairs, windows, base, own_w):
    lane = lax.broadcasted_iota(jnp.int32, (1, 128), 1)
    code = jnp.full((1, 128), -1, jnp.int32)
    numer = jnp.zeros((1, 128), jnp.int32)
    denom = jnp.ones((1, 128), jnp.int32)
    for p in range(SLOTS):
        i, j = pairs[0, p], pairs[1, p]
        live = i >= 0
        ia, ja = jnp.maximum(i, 0), jnp.maximum(j, 0)
        lo_i, hi_i = windows[0, ia], windows[1, ia]
        lo_j, hi_j = windows[0, ja], windows[1, ja]
        inter = jnp.maximum(jnp.minimum(hi_i, hi_j) - jnp.maximum(lo_i, lo_j), 0)
        near = i - base
        far = j - base - (p // CAP) * BLK_DEV
        here = lane == p
        code = jnp.where(here, jnp.where(live, near * BLK_DEV + far, -1), code)
        numer = jnp.where(here, jnp.where(live, inter + 16, 0), numer)
        denom = jnp.where(here, jnp.where(live, hi_i - lo_i + hi_j - lo_j + 16, 1), denom)
    weight = numer.astype(jnp.float32) / denom.astype(jnp.float32)
    row = lax.broadcasted_iota(jnp.int32, (16, 128), 0)
    wide = lax.broadcasted_iota(jnp.int32, (16, 128), 1)
    packed = jnp.zeros((16, 128), jnp.float32)
    for g in range(REACH + 1):
        hit = (row == code) & (wide // CAP == g)
        column = jnp.sum(jnp.where(hit, weight, 0.0), axis=1, keepdims=True)
        packed = jnp.where(wide // 32 == g, column, packed)
    own_w[...] = packed * (1.0 / SAMPLES)


def kernel(
    length,
    spectra, pairs_in, windows_in,
    corr, profiles,
    own, acc, z, both, stash, ahead, behind, sib_ahead, sib_behind, sib_own, own_w, far_w, pairs, windows,
    send_a, recv_a, send_b, recv_b,
    send_sa, recv_sa, send_sb, recv_sb, send_so, recv_so, send_w, recv_w, load_sem, table_sem,
):
    me = lax.axis_index("feat")
    core = lax.axis_index("samp")
    has_left, has_right = me > 0, me < length - 1
    to_left, to_right, to_sib = (me - 1, core), (me + 1, core), (me, 1 - core)

    def has_ahead(m):
        return me + 1 + m // BLK_DEV < length

    def has_behind(m):
        return me - 1 - m // BLK_DEV >= 0

    barrier = pltpu.get_barrier_semaphore()

    def greet(target):
        pl.semaphore_signal(barrier, inc=1, device_id=target, device_id_type=MESH)

    pl.when(has_left)(lambda: greet(to_left))
    pl.when(has_right)(lambda: greet(to_right))
    greet(to_sib)

    def own_chunk(b):
        return spectra.at[pl.ds(b * BS, BS), :]

    def load(b):
        return pltpu.make_async_copy(own_chunk(b), own.at[b], load_sem.at[b])

    tables = (
        pltpu.make_async_copy(pairs_in, pairs, table_sem.at[0]),
        pltpu.make_async_copy(windows_in, windows, table_sem.at[1]),
    )
    for copy in tables:
        copy.start()
    for b in range(BLK_DEV):
        load(b).start()
    pl.when(has_left & has_right)(lambda: pl.semaphore_wait(barrier, 3))
    pl.when(jnp.logical_not(has_left & has_right))(lambda: pl.semaphore_wait(barrier, 2))

    def remote(src, dst, send, recv, target):
        return pltpu.make_async_remote_copy(
            src_ref=src, dst_ref=dst, send_sem=send, recv_sem=recv,
            device_id=target, device_id_type=MESH,
        )

    def w_copy(h):
        source = own_w if h == 0 else far_w.at[h - 1]
        return remote(source, far_w.at[h], send_w.at[h], recv_w.at[h], to_right)

    def ahead_copy(m, source):
        return remote(source, ahead.at[m], send_a.at[m], recv_a.at[m], to_left)

    def behind_copy(m, source):
        return remote(source, behind.at[m], send_b.at[m], recv_b.at[m], to_right)

    def rows_of(part):
        return pl.ds(part * HALF, HALF)

    def last_copy(part):
        source = behind.at[LAST - BLK_DEV, rows_of(part), :]
        target = behind.at[LAST, rows_of(part), :]
        return remote(source, target, send_b.at[LAST + part], recv_b.at[LAST + part], to_right)

    def sib_ahead_copy(m):
        return remote(ahead.at[m], sib_ahead.at[m], send_sa.at[m], recv_sa.at[m], to_sib)

    def sib_behind_copy(m):
        return remote(behind.at[m], sib_behind.at[m], send_sb.at[m], recv_sb.at[m], to_sib)

    def sib_last_copy(part):
        source = behind.at[LAST, rows_of(part), :]
        target = sib_behind.at[LAST, rows_of(part), :]
        return remote(source, target, send_sb.at[LAST + part], recv_sb.at[LAST + part], to_sib)

    def sib_own_copy(b):
        return remote(own_chunk(b), sib_own.at[b], send_so.at[b], recv_so.at[b], to_sib)

    for b in range(BLK_DEV):
        pl.when(has_left)(lambda b=b: ahead_copy(b, own_chunk(b)).start())
        pl.when(has_right)(lambda b=b: behind_copy(b, own_chunk(b)).start())
        sib_own_copy(b).start()
    for copy in tables:
        copy.wait()
    pair_weights(pairs, windows, me * BLK_DEV, own_w)
    pl.when(has_right)(lambda: w_copy(0).start())

    def standardize(mine, other):
        x1, x2 = mine.astype(jnp.float32), other.astype(jnp.float32)
        total = jnp.sum(x1 + x2, axis=1, keepdims=True)
        squares = jnp.sum(x1 * x1 + x2 * x2, axis=1, keepdims=True)
        mean = total / SAMPLES
        var = squares / SAMPLES - mean * mean
        inv = lax.rsqrt(var + 1e-05)
        z1, z2 = (x1 - mean) * inv, (x2 - mean) * inv
        return jnp.concatenate([z1.astype(jnp.bfloat16), z2.astype(jnp.bfloat16)], axis=1)

    def gram(za, zc):
        return lax.dot_general(za, zc, NT, preferred_element_type=jnp.float32)

    def dot(x, y):
        return jnp.dot(x, y, preferred_element_type=jnp.float32)

    def rows_at(a):
        return slice(a * BS, (a + 1) * BS)

    def own_block(b, _):
        load(b).wait()
        sib_own_copy(b).wait_recv()
        zb = standardize(own[b], sib_own[b])
        rows = pl.ds(pl.multiple_of(b * BS, BS), BS)
        z[rows, :] = zb
        acc[rows, :] = zb[:, :BS].astype(jnp.float32)
        return 0

    lax.fori_loop(0, BLK_DEV, own_block, 0)

    for a in range(BLK_DEV):
        tiles = []
        for c in range(BLK_DEV):
            r = min(a, c) * BLK_DEV + max(a, c)
            tile = gram(z[rows_at(a), :], z[rows_at(c), :]) * own_w[r : r + 1, 0:1]
            if a <= c:
                stash[a * BLK_DEV + c] = tile
            tiles.append(tile.astype(jnp.bfloat16))
        acc[rows_at(a), :] += dot(jnp.concatenate(tiles, axis=1), z[:, :BS])

    def slots_of_group(g):
        def one(q, _):
            i, j = pairs[0, g * CAP + q], pairs[1, g * CAP + q]
            near = jnp.clip(i - me * BLK_DEV, 0, BLK_DEV - 1)
            far = jnp.clip(j - (me + g) * BLK_DEV, 0, BLK_DEV - 1)
            tile = stash[near * BLK_DEV + far]
            corr[(g % 2) * CAP + q] = jnp.where(i >= 0, tile, 0.0)
            return 0

        lax.fori_loop(0, CAP, one, 0)

    @pl.when(core == 0)
    def _():
        slots_of_group(0)

    def receive_ahead(k):
        @pl.when(has_ahead(k))
        def _():
            ahead_copy(k, ahead.at[k]).wait_recv()
            sib_ahead_copy(k).start()

            @pl.when(has_left & (k < HOPS - BLK_DEV))
            def _():
                ahead_copy(k + BLK_DEV, ahead.at[k]).start()

    def receive_behind(k):
        @pl.when(has_behind(k))
        def _():
            behind_copy(k, behind.at[k]).wait_recv()
            sib_behind_copy(k).start()

            @pl.when(has_right & (k < LAST - BLK_DEV))
            def _():
                behind_copy(k + BLK_DEV, behind.at[k]).start()

            @pl.when(has_right & (k == LAST - BLK_DEV))
            def _():
                last_copy(0).start()
                last_copy(1).start()

        for h in range(REACH):
            @pl.when(has_behind(k) & (k == h * BLK_DEV))
            def _():
                w_copy(h).wait_recv()
                if h < REACH - 1:
                    pl.when(has_right)(lambda: w_copy(h + 1).start())

    def receive_last(part):
        last_copy(part).wait_recv()
        sib_last_copy(part).start()

    def weight(table, row, g, there):
        picked = (lax.broadcasted_iota(jnp.int32, (1, 128), 1) // 32 == g) & there
        return jnp.max(jnp.where(picked, table[pl.ds(row, 1), :], 0.0), axis=1, keepdims=True)

    def process(m, n):
        there_a, there_b = has_ahead(m), (n >= 0) & has_behind(n)
        n = jnp.maximum(n, 0)
        g, c = m // BLK_DEV + 1, m % BLK_DEV
        h, d = n // BLK_DEV + 1, n % BLK_DEV

        @pl.when(there_a)
        def _():
            sib_ahead_copy(m).wait_recv()
            both[:BS, :] = standardize(ahead[m], sib_ahead[m])

        @pl.when(jnp.logical_not(there_a))
        def _():
            both[:BS, :] = jnp.zeros((BS, 2 * BS), jnp.bfloat16)

        @pl.when(there_b)
        def _():
            sib_behind_copy(n).wait_recv()
            both[BS:, :] = standardize(behind[n], sib_behind[n])

        @pl.when(jnp.logical_not(there_b))
        def _():
            both[BS:, :] = jnp.zeros((BS, 2 * BS), jnp.bfloat16)

        grams = gram(z[...], both[...])
        tiles = []
        for a in range(BLK_DEV):
            wa = weight(own_w, a * BLK_DEV + c, g, there_a)
            wb = weight(far_w.at[h - 1], d * BLK_DEV + a, h, there_b)
            ta, tb = grams[rows_at(a), :BS] * wa, grams[rows_at(a), BS:] * wb
            stash[a * BLK_DEV + c] = ta
            tiles.append(jnp.concatenate([ta.astype(jnp.bfloat16), tb.astype(jnp.bfloat16)], axis=1))
        acc[...] += dot(jnp.concatenate(tiles, axis=0), both[:, :BS])

        @pl.when((c == BLK_DEV - 1) & (core == g // 2) & (g < REACH))
        def _():
            slots_of_group(g)

    def add_behind(m, rows):
        block = standardize(behind[m, rows, :], sib_behind[m, rows, :])
        grams = gram(z[...], block)
        tiles = []
        for a in range(BLK_DEV):
            w = weight(far_w.at[REACH - 1], m % BLK_DEV * BLK_DEV + a, REACH, True)
            tiles.append((grams[rows_at(a), :] * w).astype(jnp.bfloat16))
        acc[...] += dot(jnp.concatenate(tiles, axis=0), block[:, :BS])

    early = me % COLUMN < COLUMN // 2

    def step(k, _):
        pl.when((k < LAST) & jnp.logical_not(early))(lambda: receive_behind(k))
        pl.when(k < HOPS)(lambda: receive_ahead(k))
        pl.when((k > 0) & (k < HOPS) & early)(lambda: receive_behind(k - 1))
        pl.when((k == HOPS) & has_behind(LAST))(lambda: receive_last(0))
        pl.when(k > 0)(lambda: process(k - 1, k - 2))
        return 0

    lax.fori_loop(0, HOPS + 1, step, 0)

    @pl.when(has_behind(LAST))
    def _():
        receive_last(1)
        sib_last_copy(0).wait_recv()
        add_behind(LAST, rows_of(0))

    @pl.when(core == REACH // 2)
    def _():
        slots_of_group(REACH)

    @pl.when(has_behind(LAST))
    def _():
        sib_last_copy(1).wait_recv()
        add_behind(LAST, rows_of(1))

    for a in range(BLK_DEV):
        profiles[a] = acc[rows_at(a), :].astype(jnp.bfloat16)

    for h in range(REACH):
        sent = has_right if h == 0 else has_right & has_behind((h - 1) * BLK_DEV)
        pl.when(sent)(lambda h=h: w_copy(h).wait_send())

    def drain(m, _):
        mine = m < BLK_DEV
        sent_a = has_left & (mine | has_ahead(m - BLK_DEV))
        sent_b = has_right & (mine | has_behind(m - BLK_DEV))
        pl.when(sent_a)(lambda: ahead_copy(m, ahead.at[m]).wait_send())
        pl.when(has_ahead(m))(lambda: sib_ahead_copy(m).wait_send())
        pl.when(sent_b & (m < LAST))(lambda: behind_copy(m, behind.at[m]).wait_send())
        pl.when(has_behind(m) & (m < LAST))(lambda: sib_behind_copy(m).wait_send())
        return 0

    lax.fori_loop(0, HOPS, drain, 0)
    for part in range(2):
        sent = has_right & has_behind(LAST - BLK_DEV)
        pl.when(sent)(lambda part=part: last_copy(part).wait_send())
        pl.when(has_behind(LAST))(lambda part=part: sib_last_copy(part).wait_send())
    for b in range(BLK_DEV):
        sib_own_copy(b).wait_send()


def write_out(corr, profiles, corr_out, profiles_out, sems):
    copies = [
        pltpu.make_async_copy(corr.at[p], corr_out.at[p], sems.at[p]) for p in range(SLOTS // 2)
    ]
    copies += [
        pltpu.make_async_copy(
            profiles.at[b], profiles_out.at[pl.ds(b * BS, BS), :], sems.at[SLOTS // 2 + b]
        )
        for b in range(BLK_DEV)
    ]
    for copy in copies:
        copy.start()
    for copy in copies:
        copy.wait()


def body(spectra, pair_blocks, windows):
    length = lax.axis_size("feat")
    rows, width = spectra.shape
    vmem, hbm = pl.BlockSpec(memory_space=pltpu.VMEM), pl.BlockSpec(memory_space=pltpu.HBM)
    anywhere = pl.BlockSpec(memory_space=pl.ANY)
    chunks = pltpu.VMEM((HOPS, BS, BS), jnp.bfloat16)
    blocks = pltpu.VMEM((BLK_DEV, BS, BS), jnp.bfloat16)
    many = pltpu.SemaphoreType.DMA((HOPS,))
    more = pltpu.SemaphoreType.DMA((HOPS + 1,))
    few = pltpu.SemaphoreType.DMA((BLK_DEV,))
    corr, profiles = pl.pallas_call(
        functools.partial(kernel, length),
        out_shape=(
            jax.ShapeDtypeStruct((SLOTS // 2, BS, BS), jnp.float32),
            jax.ShapeDtypeStruct((BLK_DEV, BS, BS), jnp.bfloat16),
        ),
        in_specs=[hbm, hbm, hbm],
        out_specs=(vmem, vmem),
        scratch_shapes=[
            blocks,
            pltpu.VMEM((BLK_DEV * BS, BS), jnp.float32),
            pltpu.VMEM((BLK_DEV * BS, 2 * BS), jnp.bfloat16),
            pltpu.VMEM((2 * BS, 2 * BS), jnp.bfloat16),
            pltpu.VMEM((BLK_DEV * BLK_DEV, BS, BS), jnp.float32),
            chunks, chunks, chunks, chunks, blocks,
            pltpu.VMEM((16, 128), jnp.float32),
            pltpu.VMEM((REACH, 16, 128), jnp.float32),
            pltpu.SMEM((2, SLOTS), jnp.int32),
            pltpu.SMEM((2, windows.shape[0]), jnp.int32),
            many, many, more, more,
            many, many, more, more,
            few, few,
            pltpu.SemaphoreType.DMA((REACH,)), pltpu.SemaphoreType.DMA((REACH,)),
            few, pltpu.SemaphoreType.DMA((2,)),
        ],
        compiler_params=pltpu.CompilerParams(
            collective_id=0, has_side_effects=True, vmem_limit_bytes=40 << 20
        ),
    )(*(pltpu.with_memory_space_constraint(x, pltpu.HBM) for x in (spectra, pair_blocks.T, windows.T)))
    return pl.pallas_call(
        write_out,
        out_shape=(
            jax.ShapeDtypeStruct(corr.shape, corr.dtype),
            jax.ShapeDtypeStruct((rows, width), jnp.bfloat16),
        ),
        in_specs=[anywhere, anywhere],
        out_specs=(hbm, hbm),
        scratch_shapes=[pltpu.SemaphoreType.DMA((SLOTS // 2 + BLK_DEV,))],
        compiler_params=pltpu.CompilerParams(vmem_limit_bytes=1 << 20),
    )(corr, profiles)


def solution(mesh):
    placed = (P("feat", "samp"), P("feat", None), P())
    return jax.shard_map(
        body,
        mesh=mesh,
        in_specs=placed,
        out_specs=(P(("feat", "samp"), None, None), P("feat", "samp")),
        check_vma=False,
    )
```

```python
import functools

import jax
import jax.numpy as jnp
from jax import lax
from jax.experimental import pallas as pl
from jax.experimental.pallas import tpu as pltpu
from jax.sharding import PartitionSpec as P

BS = 256
BLK_DEV = 4
CAP = 8
REACH = 3
SLOTS = 32
HOPS = REACH * BLK_DEV
LAST = HOPS - 1
HALF = BS // 2
COLUMN = 8
DRAIN = 5
SAMPLES = 512
MESH = pl.DeviceIdType.MESH
NT = (((1,), (1,)), ((), ()))


def pair_weights(pairs, windows, base, own_w):
    row = lax.broadcasted_iota(jnp.int32, (CAP, 128), 0)
    lane = lax.broadcasted_iota(jnp.int32, (CAP, 128), 1)
    total = jnp.zeros((1, 128), jnp.float32)
    for g in range(REACH + 1):
        place = jnp.full((CAP, 128), -1, jnp.int32)
        numer = jnp.zeros((CAP, 128), jnp.int32)
        denom = jnp.ones((CAP, 128), jnp.int32)
        for q in range(CAP):
            i, j = pairs[0, g * CAP + q], pairs[1, g * CAP + q]
            live = i >= 0
            ia, ja = jnp.maximum(i, 0), jnp.maximum(j, 0)
            lo_i, hi_i = windows[0, ia], windows[1, ia]
            lo_j, hi_j = windows[0, ja], windows[1, ja]
            inter = jnp.maximum(jnp.minimum(hi_i, hi_j) - jnp.maximum(lo_i, lo_j), 0)
            code = (i - base) * BLK_DEV + j - base - g * BLK_DEV + g * BLK_DEV * BLK_DEV
            here = row == q
            place = jnp.where(here, jnp.where(live, code, -1), place)
            numer = jnp.where(here, jnp.where(live, inter + 16, 0), numer)
            denom = jnp.where(here, jnp.where(live, hi_i - lo_i + hi_j - lo_j + 16, 1), denom)
        weight = numer.astype(jnp.float32) / denom.astype(jnp.float32)
        total += jnp.sum(jnp.where(lane == place, weight, 0.0), axis=0, keepdims=True)
    own_w[...] = total * (1.0 / SAMPLES)


def kernel(
    length,
    spectra, pairs_in, windows_in,
    corr, profiles,
    own, acc, z, both, stash, ahead, behind, sib_ahead, sib_behind, sib_own, own_w, far_w, pairs, windows,
    send_a, recv_a, send_b, recv_b,
    send_sa, recv_sa, send_sb, recv_sb, send_so, recv_so, send_w, recv_w, load_sem, table_sem,
):
    me = lax.axis_index("feat")
    core = lax.axis_index("samp")
    has_left, has_right = me > 0, me < length - 1
    to_left, to_right, to_sib = (me - 1, core), (me + 1, core), (me, 1 - core)

    def has_ahead(m):
        return me + 1 + m // BLK_DEV < length

    def has_behind(m):
        return me - 1 - m // BLK_DEV >= 0

    barrier = pltpu.get_barrier_semaphore()

    def greet(target):
        pl.semaphore_signal(barrier, inc=1, device_id=target, device_id_type=MESH)

    pl.when(has_left)(lambda: greet(to_left))
    pl.when(has_right)(lambda: greet(to_right))
    greet(to_sib)

    def own_chunk(b):
        return spectra.at[pl.ds(b * BS, BS), :]

    def load(b):
        return pltpu.make_async_copy(own_chunk(b), own.at[b], load_sem.at[b])

    tables = (
        pltpu.make_async_copy(pairs_in, pairs, table_sem.at[0]),
        pltpu.make_async_copy(windows_in, windows, table_sem.at[1]),
    )
    for copy in tables:
        copy.start()
    for b in range(BLK_DEV):
        load(b).start()
    pl.when(has_left & has_right)(lambda: pl.semaphore_wait(barrier, 3))
    pl.when(jnp.logical_not(has_left & has_right))(lambda: pl.semaphore_wait(barrier, 2))

    def remote(src, dst, send, recv, target):
        return pltpu.make_async_remote_copy(
            src_ref=src, dst_ref=dst, send_sem=send, recv_sem=recv,
            device_id=target, device_id_type=MESH,
        )

    def w_copy(h):
        source = own_w if h == 0 else far_w.at[h - 1]
        return remote(source, far_w.at[h], send_w.at[h], recv_w.at[h], to_right)

    def ahead_copy(m, source):
        return remote(source, ahead.at[m], send_a.at[m], recv_a.at[m], to_left)

    def behind_copy(m, source):
        return remote(source, behind.at[m], send_b.at[m], recv_b.at[m], to_right)

    def rows_of(part):
        return pl.ds(part * HALF, HALF)

    def last_copy(part):
        source = behind.at[LAST - BLK_DEV, rows_of(part), :]
        target = behind.at[LAST, rows_of(part), :]
        return remote(source, target, send_b.at[LAST + part], recv_b.at[LAST + part], to_right)

    def sib_ahead_copy(m):
        return remote(ahead.at[m], sib_ahead.at[m], send_sa.at[m], recv_sa.at[m], to_sib)

    def sib_behind_copy(m):
        return remote(behind.at[m], sib_behind.at[m], send_sb.at[m], recv_sb.at[m], to_sib)

    def sib_last_copy(part):
        source = behind.at[LAST, rows_of(part), :]
        target = sib_behind.at[LAST, rows_of(part), :]
        return remote(source, target, send_sb.at[LAST + part], recv_sb.at[LAST + part], to_sib)

    def sib_own_copy(b):
        return remote(own_chunk(b), sib_own.at[b], send_so.at[b], recv_so.at[b], to_sib)

    for b in range(BLK_DEV):
        pl.when(has_left)(lambda b=b: ahead_copy(b, own_chunk(b)).start())
        pl.when(has_right)(lambda b=b: behind_copy(b, own_chunk(b)).start())
        sib_own_copy(b).start()
    for copy in tables:
        copy.wait()
    pair_weights(pairs, windows, me * BLK_DEV, own_w)
    pl.when(has_right)(lambda: w_copy(0).start())

    def standardize(mine, other):
        x1, x2 = mine.astype(jnp.float32), other.astype(jnp.float32)
        total = jnp.sum(x1 + x2, axis=1, keepdims=True)
        squares = jnp.sum(x1 * x1 + x2 * x2, axis=1, keepdims=True)
        mean = total / SAMPLES
        var = squares / SAMPLES - mean * mean
        inv = lax.rsqrt(var + 1e-05)
        z1, z2 = (x1 - mean) * inv, (x2 - mean) * inv
        return jnp.concatenate([z1.astype(jnp.bfloat16), z2.astype(jnp.bfloat16)], axis=1)

    def gram(za, zc):
        return lax.dot_general(za, zc, NT, preferred_element_type=jnp.float32)

    def dot(x, y):
        return jnp.dot(x, y, preferred_element_type=jnp.float32)

    def rows_at(a):
        return slice(a * BS, (a + 1) * BS)

    def weight(table, g, a, c, there=True):
        lane = lax.broadcasted_iota(jnp.int32, (1, 128), 1)
        picked = (lane == (g * BLK_DEV + a) * BLK_DEV + c) & there
        return jnp.max(jnp.where(picked, table[...], 0.0), axis=1, keepdims=True)

    def own_block(b, _):
        load(b).wait()
        sib_own_copy(b).wait_recv()
        zb = standardize(own[b], sib_own[b])
        rows = pl.ds(pl.multiple_of(b * BS, BS), BS)
        z[rows, :] = zb
        acc[rows, :] = zb[:, :BS].astype(jnp.float32)
        return 0

    lax.fori_loop(0, BLK_DEV, own_block, 0)

    for a in range(BLK_DEV):
        tiles = []
        for c in range(BLK_DEV):
            w = weight(own_w, 0, min(a, c), max(a, c))
            tile = gram(z[rows_at(a), :], z[rows_at(c), :]) * w
            if a <= c:
                stash[a * BLK_DEV + c] = tile
            tiles.append(tile.astype(jnp.bfloat16))
        acc[rows_at(a), :] += dot(jnp.concatenate(tiles, axis=1), z[:, :BS])

    def slots_of_group(g):
        def one(q, _):
            i, j = pairs[0, g * CAP + q], pairs[1, g * CAP + q]
            near = jnp.clip(i - me * BLK_DEV, 0, BLK_DEV - 1)
            far = jnp.clip(j - (me + g) * BLK_DEV, 0, BLK_DEV - 1)
            tile = stash[near * BLK_DEV + far]
            corr[(g % 2) * CAP + q] = jnp.where(i >= 0, tile, 0.0)
            return 0

        lax.fori_loop(0, CAP, one, 0)

    @pl.when(core == 0)
    def _():
        slots_of_group(0)

    def receive_ahead(k):
        @pl.when(has_ahead(k))
        def _():
            ahead_copy(k, ahead.at[k]).wait_recv()
            sib_ahead_copy(k).start()

            @pl.when(has_left & (k < HOPS - BLK_DEV))
            def _():
                ahead_copy(k + BLK_DEV, ahead.at[k]).start()

    def receive_behind(k):
        @pl.when(has_behind(k))
        def _():
            behind_copy(k, behind.at[k]).wait_recv()
            sib_behind_copy(k).start()

            @pl.when(has_right & (k < LAST - BLK_DEV))
            def _():
                behind_copy(k + BLK_DEV, behind.at[k]).start()

            @pl.when(has_right & (k == LAST - BLK_DEV))
            def _():
                last_copy(0).start()
                last_copy(1).start()

        for h in range(REACH):
            @pl.when(has_behind(k) & (k == h * BLK_DEV))
            def _():
                w_copy(h).wait_recv()
                if h < REACH - 1:
                    pl.when(has_right)(lambda: w_copy(h + 1).start())

    def receive_last(part):
        last_copy(part).wait_recv()
        sib_last_copy(part).start()

    def process(m, n):
        there_a, there_b = has_ahead(m), (n >= 0) & has_behind(n)
        n = jnp.maximum(n, 0)
        g, c = m // BLK_DEV + 1, m % BLK_DEV
        h, d = n // BLK_DEV + 1, n % BLK_DEV

        @pl.when(there_a)
        def _():
            sib_ahead_copy(m).wait_recv()
            both[:BS, :] = standardize(ahead[m], sib_ahead[m])

        @pl.when(jnp.logical_not(there_a))
        def _():
            both[:BS, :] = jnp.zeros((BS, 2 * BS), jnp.bfloat16)

        @pl.when(there_b)
        def _():
            sib_behind_copy(n).wait_recv()
            both[BS:, :] = standardize(behind[n], sib_behind[n])

        @pl.when(jnp.logical_not(there_b))
        def _():
            both[BS:, :] = jnp.zeros((BS, 2 * BS), jnp.bfloat16)

        grams = gram(z[...], both[...])
        tiles = []
        for a in range(BLK_DEV):
            wa = weight(own_w, g, a, c, there_a)
            wb = weight(far_w.at[h - 1], h, d, a, there_b)
            ta, tb = grams[rows_at(a), :BS] * wa, grams[rows_at(a), BS:] * wb
            stash[a * BLK_DEV + c] = ta
            tiles.append(jnp.concatenate([ta.astype(jnp.bfloat16), tb.astype(jnp.bfloat16)], axis=1))
        acc[...] += dot(jnp.concatenate(tiles, axis=0), both[:, :BS])

        @pl.when((c == BLK_DEV - 1) & (core == g // 2) & (g < REACH))
        def _():
            slots_of_group(g)

    def write_profiles(total):
        for a in range(BLK_DEV):
            profiles[a] = total[rows_at(a), :].astype(jnp.bfloat16)

    def add_behind(m, rows, final=False):
        block = standardize(behind[m, rows, :], sib_behind[m, rows, :])
        grams = gram(z[...], block)
        tiles = []
        for a in range(BLK_DEV):
            w = weight(far_w.at[REACH - 1], REACH, m % BLK_DEV, a)
            tiles.append((grams[rows_at(a), :] * w).astype(jnp.bfloat16))
        total = acc[...] + dot(jnp.concatenate(tiles, axis=0), block[:, :BS])
        if final:
            write_profiles(total)
        else:
            acc[...] = total

    def drain(m):
        mine = m < BLK_DEV
        sent_a = has_left & (mine | has_ahead(m - BLK_DEV))
        sent_b = has_right & (mine | has_behind(m - BLK_DEV))
        pl.when(sent_a)(lambda: ahead_copy(m, ahead.at[m]).wait_send())
        pl.when(has_ahead(m))(lambda: sib_ahead_copy(m).wait_send())
        pl.when(sent_b & (m < LAST))(lambda: behind_copy(m, behind.at[m]).wait_send())
        pl.when(has_behind(m) & (m < LAST))(lambda: sib_behind_copy(m).wait_send())

        @pl.when(m == 0)
        def _():
            for b in range(BLK_DEV):
                sib_own_copy(b).wait_send()

    place = me % COLUMN
    early, late = place < COLUMN // 2, place >= COLUMN - 2

    def step(k, _):
        pl.when((k < LAST) & late)(lambda: receive_behind(k))
        pl.when(k < HOPS)(lambda: receive_ahead(k))
        lag = jnp.where(early, 1, 0)
        now = (k >= lag) & (k < LAST + lag) & jnp.logical_not(late)
        pl.when(now)(lambda: receive_behind(k - lag))
        pl.when((k == HOPS) & has_behind(LAST))(lambda: receive_last(0))
        pl.when(k > 0)(lambda: process(k - 1, k - 2))
        pl.when(k >= DRAIN)(lambda: drain(k - DRAIN))
        return 0

    lax.fori_loop(0, HOPS + 1, step, 0)

    @pl.when(has_behind(LAST))
    def _():
        receive_last(1)
        sib_last_copy(0).wait_recv()
        add_behind(LAST, rows_of(0))

    @pl.when(core == REACH // 2)
    def _():
        slots_of_group(REACH)

    @pl.when(has_behind(LAST))
    def _():
        sib_last_copy(1).wait_recv()
        add_behind(LAST, rows_of(1), final=True)

    pl.when(jnp.logical_not(has_behind(LAST)))(lambda: write_profiles(acc[...]))

    for m in range(HOPS + 1 - DRAIN, HOPS):
        drain(m)
    for h in range(REACH):
        sent = has_right if h == 0 else has_right & has_behind((h - 1) * BLK_DEV)
        pl.when(sent)(lambda h=h: w_copy(h).wait_send())

    for part in range(2):
        sent = has_right & has_behind(LAST - BLK_DEV)
        pl.when(sent)(lambda part=part: last_copy(part).wait_send())
        pl.when(has_behind(LAST))(lambda part=part: sib_last_copy(part).wait_send())


def write_out(corr, profiles, corr_out, profiles_out, sems):
    copies = [
        pltpu.make_async_copy(corr.at[p], corr_out.at[p], sems.at[p]) for p in range(SLOTS // 2)
    ]
    copies += [
        pltpu.make_async_copy(
            profiles.at[b], profiles_out.at[pl.ds(b * BS, BS), :], sems.at[SLOTS // 2 + b]
        )
        for b in range(BLK_DEV)
    ]
    for copy in copies:
        copy.start()
    for copy in copies:
        copy.wait()


def body(spectra, pair_blocks, windows):
    length = lax.axis_size("feat")
    rows, width = spectra.shape
    vmem, hbm = pl.BlockSpec(memory_space=pltpu.VMEM), pl.BlockSpec(memory_space=pltpu.HBM)
    anywhere = pl.BlockSpec(memory_space=pl.ANY)
    chunks = pltpu.VMEM((HOPS, BS, BS), jnp.bfloat16)
    blocks = pltpu.VMEM((BLK_DEV, BS, BS), jnp.bfloat16)
    many = pltpu.SemaphoreType.DMA((HOPS,))
    more = pltpu.SemaphoreType.DMA((HOPS + 1,))
    few = pltpu.SemaphoreType.DMA((BLK_DEV,))
    corr, profiles = pl.pallas_call(
        functools.partial(kernel, length),
        out_shape=(
            jax.ShapeDtypeStruct((SLOTS // 2, BS, BS), jnp.float32),
            jax.ShapeDtypeStruct((BLK_DEV, BS, BS), jnp.bfloat16),
        ),
        in_specs=[hbm, hbm, hbm],
        out_specs=(vmem, vmem),
        scratch_shapes=[
            blocks,
            pltpu.VMEM((BLK_DEV * BS, BS), jnp.float32),
            pltpu.VMEM((BLK_DEV * BS, 2 * BS), jnp.bfloat16),
            pltpu.VMEM((2 * BS, 2 * BS), jnp.bfloat16),
            pltpu.VMEM((BLK_DEV * BLK_DEV, BS, BS), jnp.float32),
            chunks, chunks, chunks, chunks, blocks,
            pltpu.VMEM((1, 128), jnp.float32),
            pltpu.VMEM((REACH, 1, 128), jnp.float32),
            pltpu.SMEM((2, SLOTS), jnp.int32),
            pltpu.SMEM((2, windows.shape[0]), jnp.int32),
            many, many, more, more,
            many, many, more, more,
            few, few,
            pltpu.SemaphoreType.DMA((REACH,)), pltpu.SemaphoreType.DMA((REACH,)),
            few, pltpu.SemaphoreType.DMA((2,)),
        ],
        compiler_params=pltpu.CompilerParams(
            collective_id=0, has_side_effects=True, vmem_limit_bytes=40 << 20
        ),
    )(*(pltpu.with_memory_space_constraint(x, pltpu.HBM) for x in (spectra, pair_blocks.T, windows.T)))
    return pl.pallas_call(
        write_out,
        out_shape=(
            jax.ShapeDtypeStruct(corr.shape, corr.dtype),
            jax.ShapeDtypeStruct((rows, width), jnp.bfloat16),
        ),
        in_specs=[anywhere, anywhere],
        out_specs=(hbm, hbm),
        scratch_shapes=[pltpu.SemaphoreType.DMA((SLOTS // 2 + BLK_DEV,))],
        compiler_params=pltpu.CompilerParams(vmem_limit_bytes=1 << 20),
    )(corr, profiles)


def solution(mesh):
    placed = (P("feat", "samp"), P("feat", None), P())
    return jax.shard_map(
        body,
        mesh=mesh,
        in_specs=placed,
        out_specs=(P(("feat", "samp"), None, None), P("feat", "samp")),
        check_vma=False,
    )
```

```python
import functools

import jax
import jax.numpy as jnp
from jax import lax
from jax.experimental import pallas as pl
from jax.experimental.pallas import tpu as pltpu
from jax.sharding import PartitionSpec as P

BS = 256
BLK_DEV = 4
CAP = 8
REACH = 3
SLOTS = 32
HOPS = REACH * BLK_DEV
LAST = HOPS - 1
HALF = BS // 2
COLUMN = 8
DRAIN = 5
SAMPLES = 512
MESH = pl.DeviceIdType.MESH
NT = (((1,), (1,)), ((), ()))


def pair_weights(pairs, windows, base, own_w):
    row = lax.broadcasted_iota(jnp.int32, (CAP, 128), 0)
    lane = lax.broadcasted_iota(jnp.int32, (CAP, 128), 1)
    total = jnp.zeros((1, 128), jnp.float32)
    for g in range(REACH + 1):
        place = jnp.full((CAP, 128), -1, jnp.int32)
        numer = jnp.zeros((CAP, 128), jnp.int32)
        denom = jnp.ones((CAP, 128), jnp.int32)
        for q in range(CAP):
            i, j = pairs[0, g * CAP + q], pairs[1, g * CAP + q]
            live = i >= 0
            ia, ja = jnp.maximum(i, 0), jnp.maximum(j, 0)
            lo_i, hi_i = windows[0, ia], windows[1, ia]
            lo_j, hi_j = windows[0, ja], windows[1, ja]
            inter = jnp.maximum(jnp.minimum(hi_i, hi_j) - jnp.maximum(lo_i, lo_j), 0)
            code = (i - base) * BLK_DEV + j - base - g * BLK_DEV + g * BLK_DEV * BLK_DEV
            here = row == q
            place = jnp.where(here, jnp.where(live, code, -1), place)
            numer = jnp.where(here, jnp.where(live, inter + 16, 0), numer)
            denom = jnp.where(here, jnp.where(live, hi_i - lo_i + hi_j - lo_j + 16, 1), denom)
        weight = numer.astype(jnp.float32) / denom.astype(jnp.float32)
        total += jnp.sum(jnp.where(lane == place, weight, 0.0), axis=0, keepdims=True)
    own_w[...] = total * (1.0 / SAMPLES)


def kernel(
    length,
    spectra, pairs_in, windows_in,
    corr, profiles,
    own, acc, z, both, stash, ahead, behind, sib_ahead, sib_behind, sib_own, tables_w, pairs, windows,
    send_a, recv_a, send_b, recv_b,
    send_sa, recv_sa, send_sb, recv_sb, send_so, recv_so, send_w, recv_w, load_sem, table_sem, left_in, right_in, sib_in,
):
    me = lax.axis_index("feat")
    core = lax.axis_index("samp")
    has_left, has_right = me > 0, me < length - 1

    def greets_left(d):
        return (d % COLUMN == 0) | (d % COLUMN == COLUMN - 1)

    left_greeted, right_greets = greets_left(me), greets_left(me + 1)
    to_left, to_right, to_sib = (me - 1, core), (me + 1, core), (me, 1 - core)

    def has_ahead(m):
        return me + 1 + m // BLK_DEV < length

    def has_behind(m):
        return me - 1 - m // BLK_DEV >= 0

    barrier = pltpu.get_barrier_semaphore()

    def greet(target):
        pl.semaphore_signal(barrier, inc=1, device_id=target, device_id_type=MESH)

    def tell(flag, target):
        pl.semaphore_signal(flag, inc=1, device_id=target, device_id_type=MESH)

    pl.when(has_left & left_greeted)(lambda: greet(to_left))
    pl.when(has_right & jnp.logical_not(right_greets))(lambda: greet(to_right))
    pl.when(core == 1)(lambda: greet(to_sib))

    def own_chunk(b):
        return spectra.at[pl.ds(b * BS, BS), :]

    def load(b):
        return pltpu.make_async_copy(own_chunk(b), own.at[b], load_sem.at[b])

    tables = (
        pltpu.make_async_copy(pairs_in, pairs, table_sem.at[0]),
        pltpu.make_async_copy(windows_in, windows, table_sem.at[1]),
    )
    for copy in tables:
        copy.start()
    for b in range(BLK_DEV):
        load(b).start()
    from_right = has_right & right_greets
    from_left = has_left & jnp.logical_not(left_greeted)
    one = jnp.int32(1)
    peers = from_right * one + from_left * one + (core == 0) * one
    for count in (1, 2, 3):
        pl.when(peers == count)(lambda count=count: pl.semaphore_wait(barrier, count))
    pl.when(core == 0)(lambda: tell(sib_in, to_sib))
    pl.when(from_right)(lambda: tell(left_in, to_right))
    pl.when(from_left)(lambda: tell(right_in, to_left))

    def remote(src, dst, send, recv, target):
        return pltpu.make_async_remote_copy(
            src_ref=src, dst_ref=dst, send_sem=send, recv_sem=recv,
            device_id=target, device_id_type=MESH,
        )

    def w_copy(h):
        return remote(tables_w.at[h], tables_w.at[h + 1], send_w.at[h], recv_w.at[h], to_right)

    def ahead_copy(m, source):
        return remote(source, ahead.at[m], send_a.at[m], recv_a.at[m], to_left)

    def behind_copy(m, source):
        return remote(source, behind.at[m], send_b.at[m], recv_b.at[m], to_right)

    def rows_of(part):
        return pl.ds(part * HALF, HALF)

    def last_copy(part):
        source = behind.at[LAST - BLK_DEV, rows_of(part), :]
        target = behind.at[LAST, rows_of(part), :]
        return remote(source, target, send_b.at[LAST + part], recv_b.at[LAST + part], to_right)

    def sib_ahead_copy(m):
        return remote(ahead.at[m], sib_ahead.at[m], send_sa.at[m], recv_sa.at[m], to_sib)

    def sib_behind_copy(m):
        return remote(behind.at[m], sib_behind.at[m], send_sb.at[m], recv_sb.at[m], to_sib)

    def sib_last_copy(part):
        source = behind.at[LAST, rows_of(part), :]
        target = sib_behind.at[LAST, rows_of(part), :]
        return remote(source, target, send_sb.at[LAST + part], recv_sb.at[LAST + part], to_sib)

    def sib_own_copy(b):
        return remote(own_chunk(b), sib_own.at[b], send_so.at[b], recv_so.at[b], to_sib)

    def send_ahead():
        for b in range(BLK_DEV):
            ahead_copy(b, own_chunk(b)).start()

    def send_behind():
        for b in range(BLK_DEV):
            behind_copy(b, own_chunk(b)).start()

    pl.when(from_left)(send_ahead)
    pl.when(from_right)(send_behind)
    pl.when(core == 1)(lambda: pl.semaphore_wait(sib_in, 1))
    for b in range(BLK_DEV):
        sib_own_copy(b).start()

    @pl.when(has_right & jnp.logical_not(right_greets))
    def _():
        pl.semaphore_wait(right_in, 1)
        send_behind()

    @pl.when(has_left & left_greeted)
    def _():
        pl.semaphore_wait(left_in, 1)
        send_ahead()

    for copy in tables:
        copy.wait()
    own_w = tables_w.at[0]
    pair_weights(pairs, windows, me * BLK_DEV, own_w)
    pl.when(has_right)(lambda: w_copy(0).start())

    def standardize(mine, other):
        x1, x2 = mine.astype(jnp.float32), other.astype(jnp.float32)
        total = jnp.sum(x1 + x2, axis=1, keepdims=True)
        squares = jnp.sum(x1 * x1 + x2 * x2, axis=1, keepdims=True)
        mean = total / SAMPLES
        var = squares / SAMPLES - mean * mean
        inv = lax.rsqrt(var + 1e-05)
        z1, z2 = (x1 - mean) * inv, (x2 - mean) * inv
        return jnp.concatenate([z1.astype(jnp.bfloat16), z2.astype(jnp.bfloat16)], axis=1)

    def gram(za, zc):
        return lax.dot_general(za, zc, NT, preferred_element_type=jnp.float32)

    def dot(x, y):
        return jnp.dot(x, y, preferred_element_type=jnp.float32)

    def rows_at(a):
        return slice(a * BS, (a + 1) * BS)

    def weight(table, g, a, c, there=True):
        lane = lax.broadcasted_iota(jnp.int32, (1, 128), 1)
        picked = (lane == (g * BLK_DEV + a) * BLK_DEV + c) & there
        return jnp.max(jnp.where(picked, table[...], 0.0), axis=1, keepdims=True)

    def own_block(b, _):
        load(b).wait()
        sib_own_copy(b).wait_recv()
        zb = standardize(own[b], sib_own[b])
        rows = pl.ds(pl.multiple_of(b * BS, BS), BS)
        z[rows, :] = zb
        acc[rows, :] = zb[:, :BS].astype(jnp.float32)
        return 0

    lax.fori_loop(0, BLK_DEV, own_block, 0)

    for a in range(BLK_DEV):
        tiles = []
        for c in range(BLK_DEV):
            w = weight(own_w, 0, min(a, c), max(a, c))
            tile = gram(z[rows_at(a), :], z[rows_at(c), :]) * w
            if a <= c:
                stash[a * BLK_DEV + c] = tile
            tiles.append(tile.astype(jnp.bfloat16))
        acc[rows_at(a), :] += dot(jnp.concatenate(tiles, axis=1), z[:, :BS])

    def slots_of_group(g):
        def one(q, _):
            i, j = pairs[0, g * CAP + q], pairs[1, g * CAP + q]
            near = jnp.clip(i - me * BLK_DEV, 0, BLK_DEV - 1)
            far = jnp.clip(j - (me + g) * BLK_DEV, 0, BLK_DEV - 1)
            tile = stash[near * BLK_DEV + far]
            corr[(g % 2) * CAP + q] = jnp.where(i >= 0, tile, 0.0)
            return 0

        lax.fori_loop(0, CAP, one, 0)

    @pl.when(core == 0)
    def _():
        slots_of_group(0)

    def receive_ahead(k):
        @pl.when(has_ahead(k))
        def _():
            ahead_copy(k, ahead.at[k]).wait_recv()
            sib_ahead_copy(k).start()

            @pl.when(has_left & (k < HOPS - BLK_DEV))
            def _():
                ahead_copy(k + BLK_DEV, ahead.at[k]).start()

    def receive_behind(k):
        @pl.when(has_behind(k))
        def _():
            behind_copy(k, behind.at[k]).wait_recv()
            sib_behind_copy(k).start()

            @pl.when(has_right & (k < LAST - BLK_DEV))
            def _():
                behind_copy(k + BLK_DEV, behind.at[k]).start()

            @pl.when(has_right & (k == LAST - BLK_DEV))
            def _():
                last_copy(0).start()
                last_copy(1).start()

        for h in range(REACH):
            @pl.when(has_behind(k) & (k == h * BLK_DEV))
            def _():
                w_copy(h).wait_recv()
                if h < REACH - 1:
                    pl.when(has_right)(lambda: w_copy(h + 1).start())

    def receive_last(part):
        last_copy(part).wait_recv()
        sib_last_copy(part).start()

    def process(m, n):
        there_a, there_b = has_ahead(m), (n >= 0) & has_behind(n)
        table = jnp.where(n >= 0, n // BLK_DEV + 1, 0)
        n = jnp.maximum(n, 0)
        g, c = m // BLK_DEV + 1, m % BLK_DEV
        h, d = n // BLK_DEV + 1, n % BLK_DEV

        @pl.when(there_a)
        def _():
            sib_ahead_copy(m).wait_recv()
            both[:BS, :] = standardize(ahead[m], sib_ahead[m])

        @pl.when(jnp.logical_not(there_a))
        def _():
            both[:BS, :] = jnp.zeros((BS, 2 * BS), jnp.bfloat16)

        @pl.when(there_b)
        def _():
            sib_behind_copy(n).wait_recv()
            both[BS:, :] = standardize(behind[n], sib_behind[n])

        @pl.when(jnp.logical_not(there_b))
        def _():
            both[BS:, :] = jnp.zeros((BS, 2 * BS), jnp.bfloat16)

        grams = gram(z[...], both[...])
        tiles = []
        for a in range(BLK_DEV):
            wa = weight(own_w, g, a, c, there_a)
            wb = weight(tables_w.at[table], h, d, a, there_b)
            ta, tb = grams[rows_at(a), :BS] * wa, grams[rows_at(a), BS:] * wb
            stash[a * BLK_DEV + c] = ta
            tiles.append(jnp.concatenate([ta.astype(jnp.bfloat16), tb.astype(jnp.bfloat16)], axis=1))
        acc[...] += dot(jnp.concatenate(tiles, axis=0), both[:, :BS])

        @pl.when((c == BLK_DEV - 1) & (core == g // 2) & (g < REACH))
        def _():
            slots_of_group(g)

    def write_profiles(total):
        for a in range(BLK_DEV):
            profiles[a] = total[rows_at(a), :].astype(jnp.bfloat16)

    def add_behind(m, rows, final=False):
        block = standardize(behind[m, rows, :], sib_behind[m, rows, :])
        grams = gram(z[...], block)
        tiles = []
        for a in range(BLK_DEV):
            w = weight(tables_w.at[REACH], REACH, m % BLK_DEV, a)
            tiles.append((grams[rows_at(a), :] * w).astype(jnp.bfloat16))
        total = acc[...] + dot(jnp.concatenate(tiles, axis=0), block[:, :BS])
        if final:
            write_profiles(total)
        else:
            acc[...] = total

    def drain(m):
        mine = m < BLK_DEV
        sent_a = has_left & (mine | has_ahead(m - BLK_DEV))
        sent_b = has_right & (mine | has_behind(m - BLK_DEV))
        pl.when(sent_a)(lambda: ahead_copy(m, ahead.at[m]).wait_send())
        pl.when(has_ahead(m))(lambda: sib_ahead_copy(m).wait_send())
        pl.when(sent_b & (m < LAST))(lambda: behind_copy(m, behind.at[m]).wait_send())
        pl.when(has_behind(m) & (m < LAST))(lambda: sib_behind_copy(m).wait_send())

        @pl.when(m == 0)
        def _():
            for b in range(BLK_DEV):
                sib_own_copy(b).wait_send()

    place = me % COLUMN
    early, late = place < COLUMN // 2, place >= COLUMN - 2
    lead = jnp.where(place < 2, 1, 0)

    def step(k, _):
        pl.when((k < LAST) & late)(lambda: receive_behind(k))

        @pl.when((k == LAST) & late & has_behind(LAST))
        def _():
            receive_last(0)
            receive_last(1)

        held = late & (k == LAST)
        pl.when((k + lead < HOPS) & jnp.logical_not(held))(lambda: receive_ahead(k + lead))
        lag = jnp.where(early, 1, 0)
        now = (k >= lag) & (k < LAST + lag) & jnp.logical_not(late)
        pl.when(now)(lambda: receive_behind(k - lag))
        last_turn = (k == HOPS) & has_behind(LAST)
        pl.when(last_turn & jnp.logical_not(late))(lambda: receive_last(0))

        @pl.when(last_turn & (lead == 1))
        def _():
            sib_behind_copy(LAST - 1).wait_recv()
            add_behind(LAST - 1, slice(None))

        @pl.when(last_turn & late)
        def _():
            sib_last_copy(0).wait_recv()
            sib_last_copy(1).wait_recv()
            add_behind(LAST, slice(None))

        m = k - 1 + lead
        pl.when((m >= 0) & (m < HOPS))(lambda: process(m, k - 2))
        pl.when(held)(lambda: receive_ahead(k))
        pl.when(k >= DRAIN)(lambda: drain(k - DRAIN))
        return 0

    pl.when(lead == 1)(lambda: receive_ahead(0))
    lax.fori_loop(0, HOPS + 1, step, 0)

    halves = has_behind(LAST) & jnp.logical_not(late)

    @pl.when(halves)
    def _():
        receive_last(1)
        sib_last_copy(0).wait_recv()
        add_behind(LAST, rows_of(0))

    @pl.when(core == REACH // 2)
    def _():
        slots_of_group(REACH)

    @pl.when(halves)
    def _():
        sib_last_copy(1).wait_recv()
        add_behind(LAST, rows_of(1), final=True)

    pl.when(jnp.logical_not(halves))(lambda: write_profiles(acc[...]))

    for m in range(HOPS + 1 - DRAIN, HOPS):
        drain(m)
    for h in range(REACH):
        sent = has_right if h == 0 else has_right & has_behind((h - 1) * BLK_DEV)
        pl.when(sent)(lambda h=h: w_copy(h).wait_send())

    for part in range(2):
        sent = has_right & has_behind(LAST - BLK_DEV)
        pl.when(sent)(lambda part=part: last_copy(part).wait_send())
        pl.when(has_behind(LAST))(lambda part=part: sib_last_copy(part).wait_send())


def write_out(corr, profiles, corr_out, profiles_out, sems):
    copies = [
        pltpu.make_async_copy(corr.at[p], corr_out.at[p], sems.at[p]) for p in range(SLOTS // 2)
    ]
    copies += [
        pltpu.make_async_copy(
            profiles.at[b], profiles_out.at[pl.ds(b * BS, BS), :], sems.at[SLOTS // 2 + b]
        )
        for b in range(BLK_DEV)
    ]
    for copy in copies:
        copy.start()
    for copy in copies:
        copy.wait()


def body(spectra, pair_blocks, windows):
    length = lax.axis_size("feat")
    rows, width = spectra.shape
    vmem, hbm = pl.BlockSpec(memory_space=pltpu.VMEM), pl.BlockSpec(memory_space=pltpu.HBM)
    anywhere = pl.BlockSpec(memory_space=pl.ANY)
    chunks = pltpu.VMEM((HOPS, BS, BS), jnp.bfloat16)
    blocks = pltpu.VMEM((BLK_DEV, BS, BS), jnp.bfloat16)
    many = pltpu.SemaphoreType.DMA((HOPS,))
    more = pltpu.SemaphoreType.DMA((HOPS + 1,))
    few = pltpu.SemaphoreType.DMA((BLK_DEV,))
    corr, profiles = pl.pallas_call(
        functools.partial(kernel, length),
        out_shape=(
            jax.ShapeDtypeStruct((SLOTS // 2, BS, BS), jnp.float32),
            jax.ShapeDtypeStruct((BLK_DEV, BS, BS), jnp.bfloat16),
        ),
        in_specs=[hbm, hbm, hbm],
        out_specs=(vmem, vmem),
        scratch_shapes=[
            blocks,
            pltpu.VMEM((BLK_DEV * BS, BS), jnp.float32),
            pltpu.VMEM((BLK_DEV * BS, 2 * BS), jnp.bfloat16),
            pltpu.VMEM((2 * BS, 2 * BS), jnp.bfloat16),
            pltpu.VMEM((BLK_DEV * BLK_DEV, BS, BS), jnp.float32),
            chunks, chunks, chunks, chunks, blocks,
            pltpu.VMEM((REACH + 1, 1, 128), jnp.float32),
            pltpu.SMEM((2, SLOTS), jnp.int32),
            pltpu.SMEM((2, windows.shape[0]), jnp.int32),
            many, many, more, more,
            many, many, more, more,
            few, few,
            pltpu.SemaphoreType.DMA((REACH,)), pltpu.SemaphoreType.DMA((REACH,)),
            few, pltpu.SemaphoreType.DMA((2,)),
            pltpu.SemaphoreType.REGULAR, pltpu.SemaphoreType.REGULAR, pltpu.SemaphoreType.REGULAR,
        ],
        compiler_params=pltpu.CompilerParams(
            collective_id=0, has_side_effects=True, vmem_limit_bytes=40 << 20
        ),
    )(*(pltpu.with_memory_space_constraint(x, pltpu.HBM) for x in (spectra, pair_blocks.T, windows.T)))
    return pl.pallas_call(
        write_out,
        out_shape=(
            jax.ShapeDtypeStruct(corr.shape, corr.dtype),
            jax.ShapeDtypeStruct((rows, width), jnp.bfloat16),
        ),
        in_specs=[anywhere, anywhere],
        out_specs=(hbm, hbm),
        scratch_shapes=[pltpu.SemaphoreType.DMA((SLOTS // 2 + BLK_DEV,))],
        compiler_params=pltpu.CompilerParams(vmem_limit_bytes=1 << 20),
    )(corr, profiles)


def solution(mesh):
    placed = (P("feat", "samp"), P("feat", None), P())
    return jax.shard_map(
        body,
        mesh=mesh,
        in_specs=placed,
        out_specs=(P(("feat", "samp"), None, None), P("feat", "samp")),
        check_vma=False,
    )
```

```python
import functools

import jax
import jax.numpy as jnp
from jax import lax
from jax.experimental import pallas as pl
from jax.experimental.pallas import tpu as pltpu
from jax.sharding import PartitionSpec as P

BS = 256
BLK_DEV = 4
CAP = 8
REACH = 3
SLOTS = 32
HOPS = REACH * BLK_DEV
LAST = HOPS - 1
HALF = BS // 2
COLUMN = 8
DRAIN = 5
SAMPLES = 512
MESH = pl.DeviceIdType.MESH
NT = (((1,), (1,)), ((), ()))


def pair_weights(pairs, windows, base, own_w):
    row = lax.broadcasted_iota(jnp.int32, (CAP, 128), 0)
    lane = lax.broadcasted_iota(jnp.int32, (CAP, 128), 1)
    total = jnp.zeros((1, 128), jnp.float32)
    for g in range(REACH + 1):
        place = jnp.full((CAP, 128), -1, jnp.int32)
        numer = jnp.zeros((CAP, 128), jnp.int32)
        denom = jnp.ones((CAP, 128), jnp.int32)
        for q in range(CAP):
            i, j = pairs[0, g * CAP + q], pairs[1, g * CAP + q]
            live = i >= 0
            ia, ja = jnp.maximum(i, 0), jnp.maximum(j, 0)
            lo_i, hi_i = windows[0, ia], windows[1, ia]
            lo_j, hi_j = windows[0, ja], windows[1, ja]
            inter = jnp.maximum(jnp.minimum(hi_i, hi_j) - jnp.maximum(lo_i, lo_j), 0)
            code = (i - base) * BLK_DEV + j - base - g * BLK_DEV + g * BLK_DEV * BLK_DEV
            here = row == q
            place = jnp.where(here, jnp.where(live, code, -1), place)
            numer = jnp.where(here, jnp.where(live, inter + 16, 0), numer)
            denom = jnp.where(here, jnp.where(live, hi_i - lo_i + hi_j - lo_j + 16, 1), denom)
        weight = numer.astype(jnp.float32) / denom.astype(jnp.float32)
        total += jnp.sum(jnp.where(lane == place, weight, 0.0), axis=0, keepdims=True)
    own_w[...] = total * (1.0 / SAMPLES)


def weight(table, g, a, c, there=True):
    lane = lax.broadcasted_iota(jnp.int32, (1, 128), 1)
    picked = (lane == (g * BLK_DEV + a) * BLK_DEV + c) & there
    return jnp.max(jnp.where(picked, table[...], 0.0), axis=1, keepdims=True)


def kernel(
    length,
    spectra, pairs_in, windows_in,
    corr, acc, z, last, last_w,
    own, both, stash, ahead, behind, sib_ahead, sib_behind, sib_own, tables_w, pairs, windows,
    send_a, recv_a, send_b, recv_b,
    send_sa, recv_sa, send_sb, recv_sb, send_so, recv_so, send_w, recv_w, load_sem, table_sem, left_in, right_in, sib_in,
):
    me = lax.axis_index("feat")
    core = lax.axis_index("samp")
    has_left, has_right = me > 0, me < length - 1

    def greets_left(d):
        return (d % COLUMN == 0) | (d % COLUMN == COLUMN - 1)

    left_greeted, right_greets = greets_left(me), greets_left(me + 1)
    to_left, to_right, to_sib = (me - 1, core), (me + 1, core), (me, 1 - core)

    def has_ahead(m):
        return me + 1 + m // BLK_DEV < length

    def has_behind(m):
        return me - 1 - m // BLK_DEV >= 0

    barrier = pltpu.get_barrier_semaphore()

    def greet(target):
        pl.semaphore_signal(barrier, inc=1, device_id=target, device_id_type=MESH)

    def tell(flag, target):
        pl.semaphore_signal(flag, inc=1, device_id=target, device_id_type=MESH)

    pl.when(has_left & left_greeted)(lambda: greet(to_left))
    pl.when(has_right & jnp.logical_not(right_greets))(lambda: greet(to_right))
    pl.when(core == 1)(lambda: greet(to_sib))

    def own_chunk(b):
        return spectra.at[pl.ds(b * BS, BS), :]

    def load(b):
        return pltpu.make_async_copy(own_chunk(b), own.at[b], load_sem.at[b])

    tables = (
        pltpu.make_async_copy(pairs_in, pairs, table_sem.at[0]),
        pltpu.make_async_copy(windows_in, windows, table_sem.at[1]),
    )
    for copy in tables:
        copy.start()
    for b in range(BLK_DEV):
        load(b).start()
    from_right = has_right & right_greets
    from_left = has_left & jnp.logical_not(left_greeted)
    one = jnp.int32(1)
    peers = from_right * one + from_left * one + (core == 0) * one
    for count in (1, 2, 3):
        pl.when(peers == count)(lambda count=count: pl.semaphore_wait(barrier, count))
    pl.when(core == 0)(lambda: tell(sib_in, to_sib))
    pl.when(from_right)(lambda: tell(left_in, to_right))
    pl.when(from_left)(lambda: tell(right_in, to_left))

    def remote(src, dst, send, recv, target):
        return pltpu.make_async_remote_copy(
            src_ref=src, dst_ref=dst, send_sem=send, recv_sem=recv,
            device_id=target, device_id_type=MESH,
        )

    def w_copy(h):
        return remote(tables_w.at[h], tables_w.at[h + 1], send_w.at[h], recv_w.at[h], to_right)

    def ahead_copy(m, source):
        return remote(source, ahead.at[m], send_a.at[m], recv_a.at[m], to_left)

    def behind_copy(m, source):
        return remote(source, behind.at[m], send_b.at[m], recv_b.at[m], to_right)

    def rows_of(part):
        return pl.ds(part * HALF, HALF)

    def last_copy(part):
        source = behind.at[LAST - BLK_DEV, rows_of(part), :]
        target = behind.at[LAST, rows_of(part), :]
        return remote(source, target, send_b.at[LAST + part], recv_b.at[LAST + part], to_right)

    def sib_ahead_copy(m):
        return remote(ahead.at[m], sib_ahead.at[m], send_sa.at[m], recv_sa.at[m], to_sib)

    def sib_behind_copy(m):
        return remote(behind.at[m], sib_behind.at[m], send_sb.at[m], recv_sb.at[m], to_sib)

    def sib_last_copy(part):
        source = behind.at[LAST, rows_of(part), :]
        target = sib_behind.at[LAST, rows_of(part), :]
        return remote(source, target, send_sb.at[LAST + part], recv_sb.at[LAST + part], to_sib)

    def sib_own_copy(b):
        return remote(own_chunk(b), sib_own.at[b], send_so.at[b], recv_so.at[b], to_sib)

    def send_ahead():
        for b in range(BLK_DEV):
            ahead_copy(b, own_chunk(b)).start()

    def send_behind():
        for b in range(BLK_DEV):
            behind_copy(b, own_chunk(b)).start()

    pl.when(from_left)(send_ahead)
    pl.when(from_right)(send_behind)
    pl.when(core == 1)(lambda: pl.semaphore_wait(sib_in, 1))
    for b in range(BLK_DEV):
        sib_own_copy(b).start()

    @pl.when(has_right & jnp.logical_not(right_greets))
    def _():
        pl.semaphore_wait(right_in, 1)
        send_behind()

    @pl.when(has_left & left_greeted)
    def _():
        pl.semaphore_wait(left_in, 1)
        send_ahead()

    for copy in tables:
        copy.wait()
    own_w = tables_w.at[0]
    pair_weights(pairs, windows, me * BLK_DEV, own_w)
    pl.when(has_right)(lambda: w_copy(0).start())

    def standardize(mine, other):
        x1, x2 = mine.astype(jnp.float32), other.astype(jnp.float32)
        total = jnp.sum(x1 + x2, axis=1, keepdims=True)
        squares = jnp.sum(x1 * x1 + x2 * x2, axis=1, keepdims=True)
        mean = total / SAMPLES
        var = squares / SAMPLES - mean * mean
        inv = lax.rsqrt(var + 1e-05)
        z1, z2 = (x1 - mean) * inv, (x2 - mean) * inv
        return jnp.concatenate([z1.astype(jnp.bfloat16), z2.astype(jnp.bfloat16)], axis=1)

    def gram(za, zc):
        return lax.dot_general(za, zc, NT, preferred_element_type=jnp.float32)

    def dot(x, y):
        return jnp.dot(x, y, preferred_element_type=jnp.float32)

    def rows_at(a):
        return slice(a * BS, (a + 1) * BS)

    def own_block(b, _):
        load(b).wait()
        sib_own_copy(b).wait_recv()
        zb = standardize(own[b], sib_own[b])
        rows = pl.ds(pl.multiple_of(b * BS, BS), BS)
        z[rows, :] = zb
        acc[rows, :] = zb[:, :BS].astype(jnp.float32)
        return 0

    lax.fori_loop(0, BLK_DEV, own_block, 0)

    for a in range(BLK_DEV):
        tiles = []
        for c in range(BLK_DEV):
            w = weight(own_w, 0, min(a, c), max(a, c))
            tile = gram(z[rows_at(a), :], z[rows_at(c), :]) * w
            if a <= c:
                stash[a * BLK_DEV + c] = tile
            tiles.append(tile.astype(jnp.bfloat16))
        acc[rows_at(a), :] += dot(jnp.concatenate(tiles, axis=1), z[:, :BS])

    def slots_of_group(g):
        def one(q, _):
            i, j = pairs[0, g * CAP + q], pairs[1, g * CAP + q]
            near = jnp.clip(i - me * BLK_DEV, 0, BLK_DEV - 1)
            far = jnp.clip(j - (me + g) * BLK_DEV, 0, BLK_DEV - 1)
            tile = stash[near * BLK_DEV + far]
            corr[(g % 2) * CAP + q] = jnp.where(i >= 0, tile, 0.0)
            return 0

        lax.fori_loop(0, CAP, one, 0)

    @pl.when(core == 0)
    def _():
        slots_of_group(0)

    def receive_ahead(k):
        @pl.when(has_ahead(k))
        def _():
            ahead_copy(k, ahead.at[k]).wait_recv()
            sib_ahead_copy(k).start()

            @pl.when(has_left & (k < HOPS - BLK_DEV))
            def _():
                ahead_copy(k + BLK_DEV, ahead.at[k]).start()

    def receive_behind(k):
        @pl.when(has_behind(k))
        def _():
            behind_copy(k, behind.at[k]).wait_recv()
            sib_behind_copy(k).start()

            @pl.when(has_right & (k < LAST - BLK_DEV))
            def _():
                behind_copy(k + BLK_DEV, behind.at[k]).start()

            @pl.when(has_right & (k == LAST - BLK_DEV))
            def _():
                last_copy(0).start()
                last_copy(1).start()

        for h in range(REACH):
            @pl.when(has_behind(k) & (k == h * BLK_DEV))
            def _():
                w_copy(h).wait_recv()
                if h < REACH - 1:
                    pl.when(has_right)(lambda: w_copy(h + 1).start())

    def receive_last(part):
        last_copy(part).wait_recv()
        sib_last_copy(part).start()

    def process(m, n):
        there_a, there_b = has_ahead(m), (n >= 0) & has_behind(n)
        table = jnp.where(n >= 0, n // BLK_DEV + 1, 0)
        n = jnp.maximum(n, 0)
        g, c = m // BLK_DEV + 1, m % BLK_DEV
        h, d = n // BLK_DEV + 1, n % BLK_DEV

        @pl.when(there_a)
        def _():
            sib_ahead_copy(m).wait_recv()
            both[:BS, :] = standardize(ahead[m], sib_ahead[m])

        @pl.when(jnp.logical_not(there_a))
        def _():
            both[:BS, :] = jnp.zeros((BS, 2 * BS), jnp.bfloat16)

        @pl.when(there_b)
        def _():
            pl.when(n < LAST)(lambda: sib_behind_copy(n).wait_recv())

            @pl.when(n == LAST)
            def _():
                sib_last_copy(0).wait_recv()
                sib_last_copy(1).wait_recv()

            both[BS:, :] = standardize(behind[n], sib_behind[n])

        @pl.when(jnp.logical_not(there_b))
        def _():
            both[BS:, :] = jnp.zeros((BS, 2 * BS), jnp.bfloat16)

        grams = gram(z[...], both[...])
        tiles = []
        for a in range(BLK_DEV):
            wa = weight(own_w, g, a, c, there_a)
            wb = weight(tables_w.at[table], h, d, a, there_b)
            ta, tb = grams[rows_at(a), :BS] * wa, grams[rows_at(a), BS:] * wb
            stash[a * BLK_DEV + c] = ta
            tiles.append(jnp.concatenate([ta.astype(jnp.bfloat16), tb.astype(jnp.bfloat16)], axis=1))
        acc[...] += dot(jnp.concatenate(tiles, axis=0), both[:, :BS])

        @pl.when((c == BLK_DEV - 1) & (core == g // 2) & (g < REACH))
        def _():
            slots_of_group(g)

    def add_behind(m, rows):
        block = standardize(behind[m, rows, :], sib_behind[m, rows, :])
        grams = gram(z[...], block)
        tiles = []
        for a in range(BLK_DEV):
            w = weight(tables_w.at[REACH], REACH, m % BLK_DEV, a)
            tiles.append((grams[rows_at(a), :] * w).astype(jnp.bfloat16))
        acc[...] += dot(jnp.concatenate(tiles, axis=0), block[:, :BS])

    def drain(m):
        mine = m < BLK_DEV
        sent_a = has_left & (mine | has_ahead(m - BLK_DEV))
        sent_b = has_right & (mine | has_behind(m - BLK_DEV))
        pl.when(sent_a)(lambda: ahead_copy(m, ahead.at[m]).wait_send())
        pl.when(has_ahead(m))(lambda: sib_ahead_copy(m).wait_send())
        pl.when(sent_b & (m < LAST))(lambda: behind_copy(m, behind.at[m]).wait_send())
        pl.when(has_behind(m) & (m < LAST))(lambda: sib_behind_copy(m).wait_send())

        @pl.when(m == 0)
        def _():
            for b in range(BLK_DEV):
                sib_own_copy(b).wait_send()

    place = me % COLUMN
    early, late = place < COLUMN // 2, place >= COLUMN - 2
    lead = jnp.where(place < 2, 1, 0)

    def step(k, _):
        pl.when((k < LAST) & late)(lambda: receive_behind(k))

        @pl.when((k == LAST) & late & has_behind(LAST))
        def _():
            receive_last(0)
            receive_last(1)

        pl.when(k + lead < HOPS)(lambda: receive_ahead(k + lead))
        lag = jnp.where(early, 1, 0)
        now = (k >= lag) & (k < LAST + lag) & jnp.logical_not(late)
        pl.when(now)(lambda: receive_behind(k - lag))
        last_turn = (k == HOPS) & has_behind(LAST)
        pl.when(last_turn & jnp.logical_not(late))(lambda: receive_last(0))

        @pl.when(last_turn & (lead == 1))
        def _():
            sib_behind_copy(LAST - 1).wait_recv()
            add_behind(LAST - 1, slice(None))

        m = k - 1 + lead
        pl.when((m >= 0) & (m < HOPS))(lambda: process(m, jnp.where(late, k - 1, k - 2)))
        pl.when(k >= DRAIN)(lambda: drain(k - DRAIN))
        return 0

    pl.when(lead == 1)(lambda: receive_ahead(0))
    lax.fori_loop(0, HOPS + 1, step, 0)

    halves = has_behind(LAST) & jnp.logical_not(late)

    pl.when(halves)(lambda: receive_last(1))

    @pl.when(core == REACH // 2)
    def _():
        slots_of_group(REACH)

    @pl.when(halves)
    def _():
        sib_last_copy(0).wait_recv()
        sib_last_copy(1).wait_recv()
        last[...] = standardize(behind[LAST], sib_behind[LAST])
        last_w[...] = tables_w[REACH]

    @pl.when(jnp.logical_not(halves))
    def _():
        last[...] = jnp.zeros((BS, 2 * BS), jnp.bfloat16)
        last_w[...] = jnp.zeros((1, 128), jnp.float32)

    for m in range(HOPS + 1 - DRAIN, HOPS):
        drain(m)
    for h in range(REACH):
        sent = has_right if h == 0 else has_right & has_behind((h - 1) * BLK_DEV)
        pl.when(sent)(lambda h=h: w_copy(h).wait_send())

    for part in range(2):
        sent = has_right & has_behind(LAST - BLK_DEV)
        pl.when(sent)(lambda part=part: last_copy(part).wait_send())
        pl.when(has_behind(LAST))(lambda part=part: sib_last_copy(part).wait_send())


def write_out(corr, acc, z, last, last_w, corr_out, profiles_out, profiles, sems):
    tiles_out = [
        pltpu.make_async_copy(corr.at[p], corr_out.at[p], sems.at[p]) for p in range(SLOTS // 2)
    ]
    rows_out = [
        pltpu.make_async_copy(
            profiles.at[b], profiles_out.at[pl.ds(b * BS, BS), :], sems.at[SLOTS // 2 + b]
        )
        for b in range(BLK_DEV)
    ]
    for copy in tiles_out:
        copy.start()
    grams = lax.dot_general(z[...], last[...], NT, preferred_element_type=jnp.float32)
    for a in range(BLK_DEV):
        rows = slice(a * BS, (a + 1) * BS)
        w = weight(last_w, REACH, BLK_DEV - 1, a)
        tile = (grams[rows, :] * w).astype(jnp.bfloat16)
        term = jnp.dot(tile, last[:, :BS], preferred_element_type=jnp.float32)
        profiles[a] = (acc[rows, :] + term).astype(jnp.bfloat16)
        rows_out[a].start()
    for copy in tiles_out + rows_out:
        copy.wait()


def body(spectra, pair_blocks, windows):
    length = lax.axis_size("feat")
    rows, width = spectra.shape
    vmem, hbm = pl.BlockSpec(memory_space=pltpu.VMEM), pl.BlockSpec(memory_space=pltpu.HBM)
    anywhere = pl.BlockSpec(memory_space=pl.ANY)
    chunks = pltpu.VMEM((HOPS, BS, BS), jnp.bfloat16)
    blocks = pltpu.VMEM((BLK_DEV, BS, BS), jnp.bfloat16)
    many = pltpu.SemaphoreType.DMA((HOPS,))
    more = pltpu.SemaphoreType.DMA((HOPS + 1,))
    few = pltpu.SemaphoreType.DMA((BLK_DEV,))
    results = pl.pallas_call(
        functools.partial(kernel, length),
        out_shape=(
            jax.ShapeDtypeStruct((SLOTS // 2, BS, BS), jnp.float32),
            jax.ShapeDtypeStruct((rows, width), jnp.float32),
            jax.ShapeDtypeStruct((rows, 2 * width), jnp.bfloat16),
            jax.ShapeDtypeStruct((BS, 2 * width), jnp.bfloat16),
            jax.ShapeDtypeStruct((1, 128), jnp.float32),
        ),
        in_specs=[hbm, hbm, hbm],
        out_specs=(vmem,) * 5,
        scratch_shapes=[
            blocks,
            pltpu.VMEM((2 * BS, 2 * BS), jnp.bfloat16),
            pltpu.VMEM((BLK_DEV * BLK_DEV, BS, BS), jnp.float32),
            chunks, chunks, chunks, chunks, blocks,
            pltpu.VMEM((REACH + 1, 1, 128), jnp.float32),
            pltpu.SMEM((2, SLOTS), jnp.int32),
            pltpu.SMEM((2, windows.shape[0]), jnp.int32),
            many, many, more, more,
            many, many, more, more,
            few, few,
            pltpu.SemaphoreType.DMA((REACH,)), pltpu.SemaphoreType.DMA((REACH,)),
            few, pltpu.SemaphoreType.DMA((2,)),
            pltpu.SemaphoreType.REGULAR, pltpu.SemaphoreType.REGULAR, pltpu.SemaphoreType.REGULAR,
        ],
        compiler_params=pltpu.CompilerParams(
            collective_id=0, has_side_effects=True, vmem_limit_bytes=40 << 20
        ),
    )(*(pltpu.with_memory_space_constraint(x, pltpu.HBM) for x in (spectra, pair_blocks.T, windows.T)))
    return pl.pallas_call(
        write_out,
        out_shape=(
            jax.ShapeDtypeStruct(results[0].shape, results[0].dtype),
            jax.ShapeDtypeStruct((rows, width), jnp.bfloat16),
        ),
        in_specs=[anywhere, vmem, vmem, vmem, vmem],
        out_specs=(hbm, hbm),
        scratch_shapes=[blocks, pltpu.SemaphoreType.DMA((SLOTS // 2 + BLK_DEV,))],
        compiler_params=pltpu.CompilerParams(vmem_limit_bytes=16 << 20),
    )(*results)


def solution(mesh):
    placed = (P("feat", "samp"), P("feat", None), P())
    return jax.shard_map(
        body,
        mesh=mesh,
        in_specs=placed,
        out_specs=(P(("feat", "samp"), None, None), P("feat", "samp")),
        check_vma=False,
    )
```

```python
import functools

import jax
import jax.numpy as jnp
from jax import lax
from jax.experimental import pallas as pl
from jax.experimental.pallas import tpu as pltpu
from jax.sharding import PartitionSpec as P

BS = 256
BLK_DEV = 4
CAP = 8
REACH = 3
SLOTS = 32
HOPS = REACH * BLK_DEV
LAST = HOPS - 1
HALF = BS // 2
COLUMN = 8
DRAIN = 5
SAMPLES = 512
MESH = pl.DeviceIdType.MESH
NT = (((1,), (1,)), ((), ()))


def pair_weights(pairs, windows, base, own_w):
    row = lax.broadcasted_iota(jnp.int32, (CAP, 128), 0)
    lane = lax.broadcasted_iota(jnp.int32, (CAP, 128), 1)
    total = jnp.zeros((1, 128), jnp.float32)
    for g in range(REACH + 1):
        place = jnp.full((CAP, 128), -1, jnp.int32)
        numer = jnp.zeros((CAP, 128), jnp.int32)
        denom = jnp.ones((CAP, 128), jnp.int32)
        for q in range(CAP):
            i, j = pairs[0, g * CAP + q], pairs[1, g * CAP + q]
            live = i >= 0
            ia, ja = jnp.maximum(i, 0), jnp.maximum(j, 0)
            lo_i, hi_i = windows[0, ia], windows[1, ia]
            lo_j, hi_j = windows[0, ja], windows[1, ja]
            inter = jnp.maximum(jnp.minimum(hi_i, hi_j) - jnp.maximum(lo_i, lo_j), 0)
            code = (i - base) * BLK_DEV + j - base - g * BLK_DEV + g * BLK_DEV * BLK_DEV
            here = row == q
            place = jnp.where(here, jnp.where(live, code, -1), place)
            numer = jnp.where(here, jnp.where(live, inter + 16, 0), numer)
            denom = jnp.where(here, jnp.where(live, hi_i - lo_i + hi_j - lo_j + 16, 1), denom)
        weight = numer.astype(jnp.float32) / denom.astype(jnp.float32)
        total += jnp.sum(jnp.where(lane == place, weight, 0.0), axis=0, keepdims=True)
    own_w[...] = total * (1.0 / SAMPLES)


def weight(table, g, a, c, there=True):
    lane = lax.broadcasted_iota(jnp.int32, (1, 128), 1)
    picked = (lane == (g * BLK_DEV + a) * BLK_DEV + c) & there
    return jnp.max(jnp.where(picked, table[...], 0.0), axis=1, keepdims=True)


def standardize(mine, other):
    x1, x2 = mine.astype(jnp.float32), other.astype(jnp.float32)
    total = jnp.sum(x1 + x2, axis=1, keepdims=True)
    squares = jnp.sum(x1 * x1 + x2 * x2, axis=1, keepdims=True)
    mean = total / SAMPLES
    var = squares / SAMPLES - mean * mean
    inv = lax.rsqrt(var + 1e-05)
    z1, z2 = (x1 - mean) * inv, (x2 - mean) * inv
    return jnp.concatenate([z1.astype(jnp.bfloat16), z2.astype(jnp.bfloat16)], axis=1)


def kernel(
    length,
    spectra, pairs_in, windows_in,
    corr, acc, z, last, last_w,
    own, both, stash, ahead, behind, sib_ahead, sib_behind, sib_own, tables_w, pairs, windows,
    send_a, recv_a, send_b, recv_b,
    send_sa, recv_sa, send_sb, recv_sb, send_so, recv_so, send_w, recv_w, load_sem, table_sem, left_in, right_in, sib_in,
):
    me = lax.axis_index("feat")
    core = lax.axis_index("samp")
    has_left, has_right = me > 0, me < length - 1

    def greets_left(d):
        return (d % COLUMN == 0) | (d % COLUMN == COLUMN - 1)

    left_greeted, right_greets = greets_left(me), greets_left(me + 1)
    to_left, to_right, to_sib = (me - 1, core), (me + 1, core), (me, 1 - core)

    def has_ahead(m):
        return me + 1 + m // BLK_DEV < length

    def has_behind(m):
        return me - 1 - m // BLK_DEV >= 0

    barrier = pltpu.get_barrier_semaphore()

    def greet(target):
        pl.semaphore_signal(barrier, inc=1, device_id=target, device_id_type=MESH)

    def tell(flag, target):
        pl.semaphore_signal(flag, inc=1, device_id=target, device_id_type=MESH)

    pl.when(has_left & left_greeted)(lambda: greet(to_left))
    pl.when(has_right & jnp.logical_not(right_greets))(lambda: greet(to_right))
    pl.when(core == 1)(lambda: greet(to_sib))

    def own_chunk(b):
        return spectra.at[pl.ds(b * BS, BS), :]

    def load(b):
        return pltpu.make_async_copy(own_chunk(b), own.at[b], load_sem.at[b])

    tables = (
        pltpu.make_async_copy(pairs_in, pairs, table_sem.at[0]),
        pltpu.make_async_copy(windows_in, windows, table_sem.at[1]),
    )
    for copy in tables:
        copy.start()
    for b in range(BLK_DEV):
        load(b).start()
    from_right = has_right & right_greets
    from_left = has_left & jnp.logical_not(left_greeted)
    one = jnp.int32(1)
    peers = from_right * one + from_left * one + (core == 0) * one
    for count in (1, 2, 3):
        pl.when(peers == count)(lambda count=count: pl.semaphore_wait(barrier, count))
    pl.when(core == 0)(lambda: tell(sib_in, to_sib))
    pl.when(from_right)(lambda: tell(left_in, to_right))
    pl.when(from_left)(lambda: tell(right_in, to_left))

    def remote(src, dst, send, recv, target):
        return pltpu.make_async_remote_copy(
            src_ref=src, dst_ref=dst, send_sem=send, recv_sem=recv,
            device_id=target, device_id_type=MESH,
        )

    def w_copy(h):
        return remote(tables_w.at[h], tables_w.at[h + 1], send_w.at[h], recv_w.at[h], to_right)

    def ahead_copy(m, source):
        return remote(source, ahead.at[m], send_a.at[m], recv_a.at[m], to_left)

    def behind_copy(m, source):
        return remote(source, behind.at[m], send_b.at[m], recv_b.at[m], to_right)

    def rows_of(part):
        return pl.ds(part * HALF, HALF)

    def last_copy(part):
        source = behind.at[LAST - BLK_DEV, rows_of(part), :]
        target = behind.at[LAST, rows_of(part), :]
        return remote(source, target, send_b.at[LAST + part], recv_b.at[LAST + part], to_right)

    def sib_ahead_copy(m):
        return remote(ahead.at[m], sib_ahead.at[m], send_sa.at[m], recv_sa.at[m], to_sib)

    def sib_behind_copy(m):
        return remote(behind.at[m], sib_behind.at[m], send_sb.at[m], recv_sb.at[m], to_sib)

    def sib_last_copy(part):
        source = behind.at[LAST, rows_of(part), :]
        target = sib_behind.at[LAST, rows_of(part), :]
        return remote(source, target, send_sb.at[LAST + part], recv_sb.at[LAST + part], to_sib)

    def sib_own_copy(b):
        return remote(own_chunk(b), sib_own.at[b], send_so.at[b], recv_so.at[b], to_sib)

    def send_ahead():
        for b in range(BLK_DEV):
            ahead_copy(b, own_chunk(b)).start()

    def send_behind():
        for b in range(BLK_DEV):
            behind_copy(b, own_chunk(b)).start()

    pl.when(from_left)(send_ahead)
    pl.when(from_right)(send_behind)
    pl.when(core == 1)(lambda: pl.semaphore_wait(sib_in, 1))
    for b in range(BLK_DEV):
        sib_own_copy(b).start()

    @pl.when(has_right & jnp.logical_not(right_greets))
    def _():
        pl.semaphore_wait(right_in, 1)
        send_behind()

    @pl.when(has_left & left_greeted)
    def _():
        pl.semaphore_wait(left_in, 1)
        send_ahead()

    for copy in tables:
        copy.wait()
    own_w = tables_w.at[0]
    pair_weights(pairs, windows, me * BLK_DEV, own_w)
    pl.when(has_right)(lambda: w_copy(0).start())

    def gram(za, zc):
        return lax.dot_general(za, zc, NT, preferred_element_type=jnp.float32)

    def dot(x, y):
        return jnp.dot(x, y, preferred_element_type=jnp.float32)

    def rows_at(a):
        return slice(a * BS, (a + 1) * BS)

    def own_block(b, _):
        load(b).wait()
        sib_own_copy(b).wait_recv()
        zb = standardize(own[b], sib_own[b])
        rows = pl.ds(pl.multiple_of(b * BS, BS), BS)
        z[rows, :] = zb
        acc[rows, :] = zb[:, :BS].astype(jnp.float32)
        return 0

    lax.fori_loop(0, BLK_DEV, own_block, 0)

    for a in range(BLK_DEV):
        tiles = []
        for c in range(BLK_DEV):
            w = weight(own_w, 0, min(a, c), max(a, c))
            tile = gram(z[rows_at(a), :], z[rows_at(c), :]) * w
            if a <= c:
                stash[a * BLK_DEV + c] = tile
            tiles.append(tile.astype(jnp.bfloat16))
        acc[rows_at(a), :] += dot(jnp.concatenate(tiles, axis=1), z[:, :BS])

    def slots_of_group(g):
        def one(q, _):
            i, j = pairs[0, g * CAP + q], pairs[1, g * CAP + q]
            near = jnp.clip(i - me * BLK_DEV, 0, BLK_DEV - 1)
            far = jnp.clip(j - (me + g) * BLK_DEV, 0, BLK_DEV - 1)
            tile = stash[near * BLK_DEV + far]
            corr[(g % 2) * CAP + q] = jnp.where(i >= 0, tile, 0.0)
            return 0

        lax.fori_loop(0, CAP, one, 0)

    @pl.when(core == 0)
    def _():
        slots_of_group(0)

    def receive_ahead(k):
        @pl.when(has_ahead(k))
        def _():
            ahead_copy(k, ahead.at[k]).wait_recv()
            sib_ahead_copy(k).start()

            @pl.when(has_left & (k < HOPS - BLK_DEV))
            def _():
                ahead_copy(k + BLK_DEV, ahead.at[k]).start()

    def receive_behind(k):
        @pl.when(has_behind(k))
        def _():
            behind_copy(k, behind.at[k]).wait_recv()
            sib_behind_copy(k).start()

            @pl.when(has_right & (k < LAST - BLK_DEV))
            def _():
                behind_copy(k + BLK_DEV, behind.at[k]).start()

            @pl.when(has_right & (k == LAST - BLK_DEV))
            def _():
                last_copy(0).start()
                last_copy(1).start()

        for h in range(REACH):
            @pl.when(has_behind(k) & (k == h * BLK_DEV))
            def _():
                w_copy(h).wait_recv()
                if h < REACH - 1:
                    pl.when(has_right)(lambda: w_copy(h + 1).start())

    def receive_last(part):
        last_copy(part).wait_recv()
        sib_last_copy(part).start()

    def process(m, n):
        there_a, there_b = has_ahead(m), (n >= 0) & has_behind(n)
        table = jnp.where(n >= 0, n // BLK_DEV + 1, 0)
        n = jnp.maximum(n, 0)
        g, c = m // BLK_DEV + 1, m % BLK_DEV
        h, d = n // BLK_DEV + 1, n % BLK_DEV

        @pl.when(there_a)
        def _():
            sib_ahead_copy(m).wait_recv()
            both[:BS, :] = standardize(ahead[m], sib_ahead[m])

        @pl.when(jnp.logical_not(there_a))
        def _():
            both[:BS, :] = jnp.zeros((BS, 2 * BS), jnp.bfloat16)

        @pl.when(there_b)
        def _():
            pl.when(n < LAST)(lambda: sib_behind_copy(n).wait_recv())

            @pl.when(n == LAST)
            def _():
                sib_last_copy(0).wait_recv()
                sib_last_copy(1).wait_recv()

            both[BS:, :] = standardize(behind[n], sib_behind[n])

        @pl.when(jnp.logical_not(there_b))
        def _():
            both[BS:, :] = jnp.zeros((BS, 2 * BS), jnp.bfloat16)

        grams = gram(z[...], both[...])
        tiles = []
        for a in range(BLK_DEV):
            wa = weight(own_w, g, a, c, there_a)
            wb = weight(tables_w.at[table], h, d, a, there_b)
            ta, tb = grams[rows_at(a), :BS] * wa, grams[rows_at(a), BS:] * wb
            stash[a * BLK_DEV + c] = ta
            tiles.append(jnp.concatenate([ta.astype(jnp.bfloat16), tb.astype(jnp.bfloat16)], axis=1))
        acc[...] += dot(jnp.concatenate(tiles, axis=0), both[:, :BS])

        @pl.when((c == BLK_DEV - 1) & (core == g // 2) & (g < REACH))
        def _():
            slots_of_group(g)

    def add_behind(m, rows):
        block = standardize(behind[m, rows, :], sib_behind[m, rows, :])
        grams = gram(z[...], block)
        tiles = []
        for a in range(BLK_DEV):
            w = weight(tables_w.at[REACH], REACH, m % BLK_DEV, a)
            tiles.append((grams[rows_at(a), :] * w).astype(jnp.bfloat16))
        acc[...] += dot(jnp.concatenate(tiles, axis=0), block[:, :BS])

    def drain(m):
        mine = m < BLK_DEV
        sent_a = has_left & (mine | has_ahead(m - BLK_DEV))
        sent_b = has_right & (mine | has_behind(m - BLK_DEV))
        pl.when(sent_a)(lambda: ahead_copy(m, ahead.at[m]).wait_send())
        pl.when(has_ahead(m))(lambda: sib_ahead_copy(m).wait_send())
        pl.when(sent_b & (m < LAST))(lambda: behind_copy(m, behind.at[m]).wait_send())
        pl.when(has_behind(m) & (m < LAST))(lambda: sib_behind_copy(m).wait_send())

        @pl.when(m == 0)
        def _():
            for b in range(BLK_DEV):
                sib_own_copy(b).wait_send()

    place = me % COLUMN
    early, late = place < COLUMN // 2, place >= COLUMN - 2
    lead = jnp.where(place < 2, 1, 0)

    def step(k, _):
        pl.when((k < LAST) & late)(lambda: receive_behind(k))

        @pl.when((k == LAST) & late & has_behind(LAST))
        def _():
            receive_last(0)
            receive_last(1)

        pl.when(k + lead < HOPS)(lambda: receive_ahead(k + lead))
        lag = jnp.where(early, 1, 0)
        now = (k >= lag) & (k < LAST + lag) & jnp.logical_not(late)
        pl.when(now)(lambda: receive_behind(k - lag))
        last_turn = (k == HOPS) & has_behind(LAST)
        pl.when(last_turn & jnp.logical_not(late))(lambda: receive_last(0))

        m = k - 1 + lead
        pl.when((m >= 0) & (m < HOPS))(lambda: process(m, jnp.where(late, k - 1, k - 2)))
        pl.when(k >= DRAIN)(lambda: drain(k - DRAIN))
        return 0

    pl.when(lead == 1)(lambda: receive_ahead(0))
    lax.fori_loop(0, HOPS + 1, step, 0)

    halves = has_behind(LAST) & jnp.logical_not(late)

    @pl.when(core == REACH // 2)
    def _():
        slots_of_group(REACH)

    pl.when(halves)(lambda: receive_last(1))

    @pl.when(halves & (lead == 1))
    def _():
        sib_behind_copy(LAST - 1).wait_recv()
        add_behind(LAST - 1, slice(None))

    @pl.when(halves)
    def _():
        sib_last_copy(0).wait_recv()
        sib_last_copy(1).wait_recv()
        last[:, :BS] = behind[LAST]
        last[:, BS:] = sib_behind[LAST]
        last_w[...] = tables_w[REACH]

    @pl.when(jnp.logical_not(halves))
    def _():
        last[...] = jnp.zeros((BS, 2 * BS), jnp.bfloat16)
        last_w[...] = jnp.zeros((1, 128), jnp.float32)

    for m in range(HOPS + 1 - DRAIN, HOPS):
        drain(m)
    for h in range(REACH):
        sent = has_right if h == 0 else has_right & has_behind((h - 1) * BLK_DEV)
        pl.when(sent)(lambda h=h: w_copy(h).wait_send())

    for part in range(2):
        sent = has_right & has_behind(LAST - BLK_DEV)
        pl.when(sent)(lambda part=part: last_copy(part).wait_send())
        pl.when(has_behind(LAST))(lambda part=part: sib_last_copy(part).wait_send())


def write_out(corr, acc, z, last, last_w, corr_out, profiles_out, profiles, sems):
    tiles_out = [
        pltpu.make_async_copy(corr.at[p], corr_out.at[p], sems.at[p]) for p in range(SLOTS // 2)
    ]
    rows_out = [
        pltpu.make_async_copy(
            profiles.at[b], profiles_out.at[pl.ds(b * BS, BS), :], sems.at[SLOTS // 2 + b]
        )
        for b in range(BLK_DEV)
    ]
    for copy in tiles_out:
        copy.start()
    block = standardize(last[:, :BS], last[:, BS:])
    grams = lax.dot_general(z[...], block, NT, preferred_element_type=jnp.float32)
    for a in range(BLK_DEV):
        rows = slice(a * BS, (a + 1) * BS)
        w = weight(last_w, REACH, BLK_DEV - 1, a)
        tile = (grams[rows, :] * w).astype(jnp.bfloat16)
        term = jnp.dot(tile, block[:, :BS], preferred_element_type=jnp.float32)
        profiles[a] = (acc[rows, :] + term).astype(jnp.bfloat16)
        rows_out[a].start()
    for copy in tiles_out + rows_out:
        copy.wait()


def body(spectra, pair_blocks, windows):
    length = lax.axis_size("feat")
    rows, width = spectra.shape
    vmem, hbm = pl.BlockSpec(memory_space=pltpu.VMEM), pl.BlockSpec(memory_space=pltpu.HBM)
    anywhere = pl.BlockSpec(memory_space=pl.ANY)
    chunks = pltpu.VMEM((HOPS, BS, BS), jnp.bfloat16)
    blocks = pltpu.VMEM((BLK_DEV, BS, BS), jnp.bfloat16)
    many = pltpu.SemaphoreType.DMA((HOPS,))
    more = pltpu.SemaphoreType.DMA((HOPS + 1,))
    few = pltpu.SemaphoreType.DMA((BLK_DEV,))
    results = pl.pallas_call(
        functools.partial(kernel, length),
        out_shape=(
            jax.ShapeDtypeStruct((SLOTS // 2, BS, BS), jnp.float32),
            jax.ShapeDtypeStruct((rows, width), jnp.float32),
            jax.ShapeDtypeStruct((rows, 2 * width), jnp.bfloat16),
            jax.ShapeDtypeStruct((BS, 2 * width), jnp.bfloat16),
            jax.ShapeDtypeStruct((1, 128), jnp.float32),
        ),
        in_specs=[hbm, hbm, hbm],
        out_specs=(vmem,) * 5,
        scratch_shapes=[
            blocks,
            pltpu.VMEM((2 * BS, 2 * BS), jnp.bfloat16),
            pltpu.VMEM((BLK_DEV * BLK_DEV, BS, BS), jnp.float32),
            chunks, chunks, chunks, chunks, blocks,
            pltpu.VMEM((REACH + 1, 1, 128), jnp.float32),
            pltpu.SMEM((2, SLOTS), jnp.int32),
            pltpu.SMEM((2, windows.shape[0]), jnp.int32),
            many, many, more, more,
            many, many, more, more,
            few, few,
            pltpu.SemaphoreType.DMA((REACH,)), pltpu.SemaphoreType.DMA((REACH,)),
            few, pltpu.SemaphoreType.DMA((2,)),
            pltpu.SemaphoreType.REGULAR, pltpu.SemaphoreType.REGULAR, pltpu.SemaphoreType.REGULAR,
        ],
        compiler_params=pltpu.CompilerParams(
            collective_id=0, has_side_effects=True, vmem_limit_bytes=40 << 20
        ),
    )(*(pltpu.with_memory_space_constraint(x, pltpu.HBM) for x in (spectra, pair_blocks.T, windows.T)))
    return pl.pallas_call(
        write_out,
        out_shape=(
            jax.ShapeDtypeStruct(results[0].shape, results[0].dtype),
            jax.ShapeDtypeStruct((rows, width), jnp.bfloat16),
        ),
        in_specs=[anywhere, vmem, vmem, vmem, vmem],
        out_specs=(hbm, hbm),
        scratch_shapes=[blocks, pltpu.SemaphoreType.DMA((SLOTS // 2 + BLK_DEV,))],
        compiler_params=pltpu.CompilerParams(vmem_limit_bytes=16 << 20),
    )(*results)


def solution(mesh):
    placed = (P("feat", "samp"), P("feat", None), P())
    return jax.shard_map(
        body,
        mesh=mesh,
        in_specs=placed,
        out_specs=(P(("feat", "samp"), None, None), P("feat", "samp")),
        check_vma=False,
    )
```

```python
import functools

import jax
import jax.numpy as jnp
from jax import lax
from jax.experimental import pallas as pl
from jax.experimental.pallas import tpu as pltpu
from jax.sharding import PartitionSpec as P

BS = 256
BLK_DEV = 4
CAP = 8
REACH = 3
SLOTS = 32
HOPS = REACH * BLK_DEV
LAST = HOPS - 1
HALF = BS // 2
COLUMN = 8
DRAIN = 4
SAMPLES = 512
MESH = pl.DeviceIdType.MESH
NT = (((1,), (1,)), ((), ()))


def pair_weights(pairs, windows, base, own_w):
    row = lax.broadcasted_iota(jnp.int32, (CAP, 128), 0)
    lane = lax.broadcasted_iota(jnp.int32, (CAP, 128), 1)
    total = jnp.zeros((1, 128), jnp.float32)
    for g in range(REACH + 1):
        place = jnp.full((CAP, 128), -1, jnp.int32)
        numer = jnp.zeros((CAP, 128), jnp.int32)
        denom = jnp.ones((CAP, 128), jnp.int32)
        for q in range(CAP):
            i, j = pairs[0, g * CAP + q], pairs[1, g * CAP + q]
            live = i >= 0
            ia, ja = jnp.maximum(i, 0), jnp.maximum(j, 0)
            lo_i, hi_i = windows[0, ia], windows[1, ia]
            lo_j, hi_j = windows[0, ja], windows[1, ja]
            inter = jnp.maximum(jnp.minimum(hi_i, hi_j) - jnp.maximum(lo_i, lo_j), 0)
            code = (i - base) * BLK_DEV + j - base - g * BLK_DEV + g * BLK_DEV * BLK_DEV
            here = row == q
            place = jnp.where(here, jnp.where(live, code, -1), place)
            numer = jnp.where(here, jnp.where(live, inter + 16, 0), numer)
            denom = jnp.where(here, jnp.where(live, hi_i - lo_i + hi_j - lo_j + 16, 1), denom)
        weight = numer.astype(jnp.float32) / denom.astype(jnp.float32)
        total += jnp.sum(jnp.where(lane == place, weight, 0.0), axis=0, keepdims=True)
    own_w[...] = total * (1.0 / SAMPLES)


def weight(table, g, a, c, there=True):
    lane = lax.broadcasted_iota(jnp.int32, (1, 128), 1)
    picked = (lane == (g * BLK_DEV + a) * BLK_DEV + c) & there
    return jnp.max(jnp.where(picked, table[...], 0.0), axis=1, keepdims=True)


def standardize(mine, other):
    x1, x2 = mine.astype(jnp.float32), other.astype(jnp.float32)
    total = jnp.sum(x1 + x2, axis=1, keepdims=True)
    squares = jnp.sum(x1 * x1 + x2 * x2, axis=1, keepdims=True)
    mean = total / SAMPLES
    var = squares / SAMPLES - mean * mean
    inv = lax.rsqrt(var + 1e-05)
    z1, z2 = (x1 - mean) * inv, (x2 - mean) * inv
    return jnp.concatenate([z1.astype(jnp.bfloat16), z2.astype(jnp.bfloat16)], axis=1)


def kernel(
    length,
    spectra, pairs_in, windows_in,
    corr, acc, z, last, last_w,
    own, both, stash, ahead, behind, sib_ahead, sib_behind, sib_own, tables_w, pairs, windows,
    send_a, recv_a, send_b, recv_b,
    send_sa, recv_sa, send_sb, recv_sb, send_so, recv_so, send_w, recv_w, load_sem, table_sem, left_in, right_in, sib_in,
):
    me = lax.axis_index("feat")
    core = lax.axis_index("samp")
    has_left, has_right = me > 0, me < length - 1

    def greets_left(d):
        return (d % COLUMN == 0) | (d % COLUMN == COLUMN - 1)

    left_greeted, right_greets = greets_left(me), greets_left(me + 1)
    to_left, to_right, to_sib = (me - 1, core), (me + 1, core), (me, 1 - core)

    def has_ahead(m):
        return me + 1 + m // BLK_DEV < length

    def has_behind(m):
        return me - 1 - m // BLK_DEV >= 0

    barrier = pltpu.get_barrier_semaphore()

    def greet(target):
        pl.semaphore_signal(barrier, inc=1, device_id=target, device_id_type=MESH)

    def tell(flag, target):
        pl.semaphore_signal(flag, inc=1, device_id=target, device_id_type=MESH)

    pl.when(has_left & left_greeted)(lambda: greet(to_left))
    pl.when(has_right & jnp.logical_not(right_greets))(lambda: greet(to_right))
    pl.when(core == 1)(lambda: greet(to_sib))

    def own_chunk(b):
        return spectra.at[pl.ds(b * BS, BS), :]

    def load(b):
        return pltpu.make_async_copy(own_chunk(b), own.at[b], load_sem.at[b])

    tables = (
        pltpu.make_async_copy(pairs_in, pairs, table_sem.at[0]),
        pltpu.make_async_copy(windows_in, windows, table_sem.at[1]),
    )
    for copy in tables:
        copy.start()
    for b in range(BLK_DEV):
        load(b).start()
    from_right = has_right & right_greets
    from_left = has_left & jnp.logical_not(left_greeted)
    one = jnp.int32(1)
    peers = from_right * one + from_left * one + (core == 0) * one
    for count in (1, 2, 3):
        pl.when(peers == count)(lambda count=count: pl.semaphore_wait(barrier, count))
    pl.when(core == 0)(lambda: tell(sib_in, to_sib))
    pl.when(from_right)(lambda: tell(left_in, to_right))
    pl.when(from_left)(lambda: tell(right_in, to_left))

    def remote(src, dst, send, recv, target):
        return pltpu.make_async_remote_copy(
            src_ref=src, dst_ref=dst, send_sem=send, recv_sem=recv,
            device_id=target, device_id_type=MESH,
        )

    def w_copy(h):
        return remote(tables_w.at[h], tables_w.at[h + 1], send_w.at[h], recv_w.at[h], to_right)

    def ahead_copy(m, source):
        return remote(source, ahead.at[m], send_a.at[m], recv_a.at[m], to_left)

    def behind_copy(m, source):
        return remote(source, behind.at[m], send_b.at[m], recv_b.at[m], to_right)

    def rows_of(part):
        return pl.ds(part * HALF, HALF)

    def last_copy(part):
        source = behind.at[LAST - BLK_DEV, rows_of(part), :]
        target = behind.at[LAST, rows_of(part), :]
        return remote(source, target, send_b.at[LAST + part], recv_b.at[LAST + part], to_right)

    def sib_ahead_copy(m):
        return remote(ahead.at[m], sib_ahead.at[m], send_sa.at[m], recv_sa.at[m], to_sib)

    def sib_behind_copy(m):
        return remote(behind.at[m], sib_behind.at[m], send_sb.at[m], recv_sb.at[m], to_sib)

    def sib_last_copy(part):
        source = behind.at[LAST, rows_of(part), :]
        target = sib_behind.at[LAST, rows_of(part), :]
        return remote(source, target, send_sb.at[LAST + part], recv_sb.at[LAST + part], to_sib)

    def sib_own_copy(b):
        return remote(own_chunk(b), sib_own.at[b], send_so.at[b], recv_so.at[b], to_sib)

    def send_ahead():
        for b in range(BLK_DEV):
            ahead_copy(b, own_chunk(b)).start()

    def send_behind():
        for b in range(BLK_DEV):
            behind_copy(b, own_chunk(b)).start()

    pl.when(from_left)(send_ahead)
    pl.when(from_right)(send_behind)
    pl.when(core == 1)(lambda: pl.semaphore_wait(sib_in, 1))
    for b in range(BLK_DEV):
        sib_own_copy(b).start()

    @pl.when(has_right & jnp.logical_not(right_greets))
    def _():
        pl.semaphore_wait(right_in, 1)
        send_behind()

    @pl.when(has_left & left_greeted)
    def _():
        pl.semaphore_wait(left_in, 1)
        send_ahead()

    for copy in tables:
        copy.wait()
    own_w = tables_w.at[0]
    pair_weights(pairs, windows, me * BLK_DEV, own_w)
    pl.when(has_right)(lambda: w_copy(0).start())

    def gram(za, zc):
        return lax.dot_general(za, zc, NT, preferred_element_type=jnp.float32)

    def dot(x, y):
        return jnp.dot(x, y, preferred_element_type=jnp.float32)

    def rows_at(a):
        return slice(a * BS, (a + 1) * BS)

    def own_block(b, _):
        load(b).wait()
        sib_own_copy(b).wait_recv()
        zb = standardize(own[b], sib_own[b])
        rows = pl.ds(pl.multiple_of(b * BS, BS), BS)
        z[rows, :] = zb
        acc[rows, :] = zb[:, :BS].astype(jnp.float32)
        return 0

    lax.fori_loop(0, BLK_DEV, own_block, 0)

    for a in range(BLK_DEV):
        tiles = []
        for c in range(BLK_DEV):
            w = weight(own_w, 0, min(a, c), max(a, c))
            tile = gram(z[rows_at(a), :], z[rows_at(c), :]) * w
            if a <= c:
                stash[a * BLK_DEV + c] = tile
            tiles.append(tile.astype(jnp.bfloat16))
        acc[rows_at(a), :] += dot(jnp.concatenate(tiles, axis=1), z[:, :BS])

    def slots_of_group(g):
        def one(q, _):
            i, j = pairs[0, g * CAP + q], pairs[1, g * CAP + q]
            near = jnp.clip(i - me * BLK_DEV, 0, BLK_DEV - 1)
            far = jnp.clip(j - (me + g) * BLK_DEV, 0, BLK_DEV - 1)
            tile = stash[near * BLK_DEV + far]
            corr[(g % 2) * CAP + q] = jnp.where(i >= 0, tile, 0.0)
            return 0

        lax.fori_loop(0, CAP, one, 0)

    @pl.when(core == 0)
    def _():
        slots_of_group(0)

    def receive_ahead(k):
        @pl.when(has_ahead(k))
        def _():
            ahead_copy(k, ahead.at[k]).wait_recv()
            sib_ahead_copy(k).start()

            @pl.when(has_left & (k < HOPS - BLK_DEV))
            def _():
                ahead_copy(k + BLK_DEV, ahead.at[k]).start()

    def receive_behind(k):
        @pl.when(has_behind(k))
        def _():
            behind_copy(k, behind.at[k]).wait_recv()
            sib_behind_copy(k).start()

            @pl.when(has_right & (k < LAST - BLK_DEV))
            def _():
                behind_copy(k + BLK_DEV, behind.at[k]).start()

            @pl.when(has_right & (k == LAST - BLK_DEV))
            def _():
                last_copy(0).start()
                last_copy(1).start()

        for h in range(REACH):
            @pl.when(has_behind(k) & (k == h * BLK_DEV))
            def _():
                w_copy(h).wait_recv()
                if h < REACH - 1:
                    pl.when(has_right)(lambda: w_copy(h + 1).start())

    def receive_last(part):
        last_copy(part).wait_recv()
        sib_last_copy(part).start()

    def process(m, n):
        there_a, there_b = has_ahead(m), (n >= 0) & has_behind(n)
        table = jnp.where(n >= 0, n // BLK_DEV + 1, 0)
        n = jnp.maximum(n, 0)
        g, c = m // BLK_DEV + 1, m % BLK_DEV
        h, d = n // BLK_DEV + 1, n % BLK_DEV

        @pl.when(there_a)
        def _():
            sib_ahead_copy(m).wait_recv()
            both[:BS, :] = standardize(ahead[m], sib_ahead[m])

        @pl.when(jnp.logical_not(there_a))
        def _():
            both[:BS, :] = jnp.zeros((BS, 2 * BS), jnp.bfloat16)

        @pl.when(there_b)
        def _():
            pl.when(n < LAST)(lambda: sib_behind_copy(n).wait_recv())

            @pl.when(n == LAST)
            def _():
                sib_last_copy(0).wait_recv()
                sib_last_copy(1).wait_recv()

            both[BS:, :] = standardize(behind[n], sib_behind[n])

        @pl.when(jnp.logical_not(there_b))
        def _():
            both[BS:, :] = jnp.zeros((BS, 2 * BS), jnp.bfloat16)

        grams = gram(z[...], both[...])
        tiles = []
        for a in range(BLK_DEV):
            wa = weight(own_w, g, a, c, there_a)
            wb = weight(tables_w.at[table], h, d, a, there_b)
            ta, tb = grams[rows_at(a), :BS] * wa, grams[rows_at(a), BS:] * wb
            stash[a * BLK_DEV + c] = ta
            tiles.append(jnp.concatenate([ta.astype(jnp.bfloat16), tb.astype(jnp.bfloat16)], axis=1))
        acc[...] += dot(jnp.concatenate(tiles, axis=0), both[:, :BS])

        @pl.when((c == BLK_DEV - 1) & (core == g // 2) & (g < REACH))
        def _():
            slots_of_group(g)

    def add_behind(m, rows):
        block = standardize(behind[m, rows, :], sib_behind[m, rows, :])
        grams = gram(z[...], block)
        tiles = []
        for a in range(BLK_DEV):
            w = weight(tables_w.at[REACH], REACH, m % BLK_DEV, a)
            tiles.append((grams[rows_at(a), :] * w).astype(jnp.bfloat16))
        acc[...] += dot(jnp.concatenate(tiles, axis=0), block[:, :BS])

    def drain(m):
        mine = m < BLK_DEV
        sent_a = has_left & (mine | has_ahead(m - BLK_DEV))
        sent_b = has_right & (mine | has_behind(m - BLK_DEV))
        pl.when(sent_a)(lambda: ahead_copy(m, ahead.at[m]).wait_send())
        pl.when(has_ahead(m))(lambda: sib_ahead_copy(m).wait_send())
        pl.when(sent_b & (m < LAST))(lambda: behind_copy(m, behind.at[m]).wait_send())
        pl.when(has_behind(m) & (m < LAST))(lambda: sib_behind_copy(m).wait_send())

        @pl.when(m == 0)
        def _():
            for b in range(BLK_DEV):
                sib_own_copy(b).wait_send()

    place = me % COLUMN
    early, late = place < COLUMN // 2, place >= COLUMN - 2
    lead = jnp.where(place < 2, 1, 0)

    def step(k, _):
        pl.when((k < LAST) & late)(lambda: receive_behind(k))

        @pl.when((k == LAST) & late & has_behind(LAST))
        def _():
            receive_last(0)
            receive_last(1)

        pl.when(k + lead < HOPS)(lambda: receive_ahead(k + lead))
        lag = jnp.where(early, 1, 0)
        now = (k >= lag) & (k < LAST + lag) & jnp.logical_not(late)
        pl.when(now)(lambda: receive_behind(k - lag))
        last_turn = (k == HOPS) & has_behind(LAST)
        pl.when(last_turn & jnp.logical_not(late))(lambda: receive_last(0))

        m = k - 1 + lead
        pl.when((m >= 0) & (m < HOPS))(lambda: process(m, jnp.where(late, k - 1, k - 2)))
        pl.when(k >= DRAIN)(lambda: drain(k - DRAIN))
        return 0

    pl.when(lead == 1)(lambda: receive_ahead(0))
    lax.fori_loop(0, HOPS + 1, step, 0)

    halves = has_behind(LAST) & jnp.logical_not(late)

    @pl.when(core == REACH // 2)
    def _():
        slots_of_group(REACH)

    pl.when(halves)(lambda: receive_last(1))

    @pl.when(halves & (lead == 1))
    def _():
        sib_behind_copy(LAST - 1).wait_recv()
        add_behind(LAST - 1, slice(None))

    @pl.when(halves)
    def _():
        sib_last_copy(0).wait_recv()
        sib_last_copy(1).wait_recv()
        last[:, :BS] = behind[LAST]
        last[:, BS:] = sib_behind[LAST]
        last_w[...] = tables_w[REACH]

    @pl.when(jnp.logical_not(halves))
    def _():
        last[...] = jnp.zeros((BS, 2 * BS), jnp.bfloat16)
        last_w[...] = jnp.zeros((1, 128), jnp.float32)

    for m in range(HOPS + 1 - DRAIN, HOPS):
        drain(m)
    for h in range(REACH):
        sent = has_right if h == 0 else has_right & has_behind((h - 1) * BLK_DEV)
        pl.when(sent)(lambda h=h: w_copy(h).wait_send())

    for part in range(2):
        sent = has_right & has_behind(LAST - BLK_DEV)
        pl.when(sent)(lambda part=part: last_copy(part).wait_send())
        pl.when(has_behind(LAST))(lambda part=part: sib_last_copy(part).wait_send())


def write_out(corr, acc, z, last, last_w, corr_out, profiles_out, profiles, sems):
    tiles_out = [
        pltpu.make_async_copy(corr.at[p], corr_out.at[p], sems.at[p]) for p in range(SLOTS // 2)
    ]
    rows_out = [
        pltpu.make_async_copy(
            profiles.at[b], profiles_out.at[pl.ds(b * BS, BS), :], sems.at[SLOTS // 2 + b]
        )
        for b in range(BLK_DEV)
    ]
    for copy in tiles_out:
        copy.start()
    block = standardize(last[:, :BS], last[:, BS:])
    grams = lax.dot_general(z[...], block, NT, preferred_element_type=jnp.float32)
    for a in range(BLK_DEV):
        rows = slice(a * BS, (a + 1) * BS)
        w = weight(last_w, REACH, BLK_DEV - 1, a)
        tile = (grams[rows, :] * w).astype(jnp.bfloat16)
        term = jnp.dot(tile, block[:, :BS], preferred_element_type=jnp.float32)
        profiles[a] = (acc[rows, :] + term).astype(jnp.bfloat16)
        rows_out[a].start()
    for copy in tiles_out + rows_out:
        copy.wait()


def body(spectra, pair_blocks, windows):
    length = lax.axis_size("feat")
    rows, width = spectra.shape
    vmem, hbm = pl.BlockSpec(memory_space=pltpu.VMEM), pl.BlockSpec(memory_space=pltpu.HBM)
    anywhere = pl.BlockSpec(memory_space=pl.ANY)
    chunks = pltpu.VMEM((HOPS, BS, BS), jnp.bfloat16)
    blocks = pltpu.VMEM((BLK_DEV, BS, BS), jnp.bfloat16)
    many = pltpu.SemaphoreType.DMA((HOPS,))
    more = pltpu.SemaphoreType.DMA((HOPS + 1,))
    few = pltpu.SemaphoreType.DMA((BLK_DEV,))
    results = pl.pallas_call(
        functools.partial(kernel, length),
        out_shape=(
            jax.ShapeDtypeStruct((SLOTS // 2, BS, BS), jnp.float32),
            jax.ShapeDtypeStruct((rows, width), jnp.float32),
            jax.ShapeDtypeStruct((rows, 2 * width), jnp.bfloat16),
            jax.ShapeDtypeStruct((BS, 2 * width), jnp.bfloat16),
            jax.ShapeDtypeStruct((1, 128), jnp.float32),
        ),
        in_specs=[hbm, hbm, hbm],
        out_specs=(vmem,) * 5,
        scratch_shapes=[
            blocks,
            pltpu.VMEM((2 * BS, 2 * BS), jnp.bfloat16),
            pltpu.VMEM((BLK_DEV * BLK_DEV, BS, BS), jnp.float32),
            chunks, chunks, chunks, chunks, blocks,
            pltpu.VMEM((REACH + 1, 1, 128), jnp.float32),
            pltpu.SMEM((2, SLOTS), jnp.int32),
            pltpu.SMEM((2, windows.shape[0]), jnp.int32),
            many, many, more, more,
            many, many, more, more,
            few, few,
            pltpu.SemaphoreType.DMA((REACH,)), pltpu.SemaphoreType.DMA((REACH,)),
            few, pltpu.SemaphoreType.DMA((2,)),
            pltpu.SemaphoreType.REGULAR, pltpu.SemaphoreType.REGULAR, pltpu.SemaphoreType.REGULAR,
        ],
        compiler_params=pltpu.CompilerParams(
            collective_id=0, has_side_effects=True, vmem_limit_bytes=40 << 20
        ),
    )(*(pltpu.with_memory_space_constraint(x, pltpu.HBM) for x in (spectra, pair_blocks.T, windows.T)))
    return pl.pallas_call(
        write_out,
        out_shape=(
            jax.ShapeDtypeStruct(results[0].shape, results[0].dtype),
            jax.ShapeDtypeStruct((rows, width), jnp.bfloat16),
        ),
        in_specs=[anywhere, vmem, vmem, vmem, vmem],
        out_specs=(hbm, hbm),
        scratch_shapes=[blocks, pltpu.SemaphoreType.DMA((SLOTS // 2 + BLK_DEV,))],
        compiler_params=pltpu.CompilerParams(vmem_limit_bytes=16 << 20),
    )(*results)


def solution(mesh):
    placed = (P("feat", "samp"), P("feat", None), P())
    return jax.shard_map(
        body,
        mesh=mesh,
        in_specs=placed,
        out_specs=(P(("feat", "samp"), None, None), P("feat", "samp")),
        check_vma=False,
    )
```
